1024 devices in a mesh: resp: 8 (over y, core), dp: 128 (over x, z).
Axes of the slice: x: 4, y: 4, z: 32, core: 2. Of those that a mesh axis runs over, the one named last changes fastest.
Arguments:
- query_in: bfloat16 [8, 128, 128, 2560], P('resp', 'dp'), may hold values from -8 to 8
- key_in: bfloat16 [8, 128, 128, 512], P('resp', 'dp'), may hold values from -8 to 8
- value_in: bfloat16 [8, 128, 128, 512], P('resp', 'dp'), may hold values from -6 to 6
- prefix_key: bfloat16 [8, 128, 256, 512], P('resp', 'dp'), may hold values from -6 to 6
- prefix_value: bfloat16 [8, 128, 256, 512], P('resp', 'dp'), may hold values from -6 to 6
- q_bias: bfloat16 [2560], replicated, may hold values from -2 to 2
- out_grad: bfloat16 [8, 128, 128, 2560], P('resp', 'dp'), may hold values from -6 to 6
- group: int32 [8, 128], P('resp', 'dp'), may hold values from 0 to 7
- resp_len: int32 [8, 128], P('resp', 'dp'), may hold values from 1 to 128
- pref_blocks: int32 [8, 128], P('resp', 'dp'), may hold values from 1 to 2
- keep: int32 [8, 128, 2], P('resp', 'dp'), may hold values 0 or 1
Outputs:
- q_grad: bfloat16 [8, 128, 128, 2560], P('resp', 'dp')
- key_grad: bfloat16 [8, 128, 128, 512], P('resp', 'dp')
- value_grad: bfloat16 [8, 128, 128, 512], P('resp', 'dp')
- prefix_key_grad: bfloat16 [8, 128, 256, 512], P('resp', 'dp')
- prefix_value_grad: bfloat16 [8, 128, 256, 512], P('resp', 'dp')
- q_bias_grad: float32 [2560], replicated
- v_bias_grad: float32 [512], replicated
The draws below stay inside these ranges and needn't reach their ends.
All inputs are finite; a program needn't handle non-finite values. No bound on the sum of `keep` on one device may be relied on, other than what follows from the above.
Results may differ from the reference program's by a relative error of at most 0.012.
The reference program's roundings to bfloat16 on the way count: a program that leaves them out, or rounds other values in their place, can miss the bound.
Values may be sent and summed in bfloat16 or wider, within the bound.
A program may use at most 64 MiB of HBM per device.

```python
import math
import jax
import jax.numpy as jnp
import numpy as np
from jax import lax

HEADS = 20
KV_HEADS = 4
HEAD_DIM = 128
BLOCK = 128
RESP_LEN = 128
PREF_BLOCKS = 2
PLEN = 256
QW = 2560
KVW = 512
HOLDERS = 8
BATCHES = 128


def drawn_parts(key):
    base_key = jax.random.fold_in(key, 11)
    key_query, key_keys, key_bias = jax.random.split(base_key, 3)
    query_shape = (HOLDERS, BATCHES, RESP_LEN, HEADS * HEAD_DIM)
    key_shape = (HOLDERS, BATCHES, RESP_LEN, KV_HEADS * HEAD_DIM)
    bias_row = jnp.clip(0.5 * jax.random.normal(key_bias, (HEADS * HEAD_DIM,), jnp.float32), -2.0, 2.0)
    queries = jnp.clip(jax.random.normal(key_query, query_shape, jnp.float32), -6.0, 6.0)
    key_rows = jnp.clip(jax.random.normal(key_keys, key_shape, jnp.float32), -6.0, 6.0)
    return (queries, key_rows, bias_row)


def draw_query_in(key, part):
    return drawn_parts(key)[0].astype(jnp.bfloat16)


def draw_key_in(key, part):
    return drawn_parts(key)[1].astype(jnp.bfloat16)


def draw_q_bias(key, part):
    return drawn_parts(key)[2].astype(jnp.bfloat16)


def touch_ends(drawn, own_key, least, largest):
    longest = drawn.shape.index(max(drawn.shape))
    spots = []
    for shift in (0, 1):
        where = [jax.random.randint(jax.random.fold_in(own_key, axis), (), 0, length) for axis, length in enumerate(drawn.shape)]
        where[longest] = (where[longest] + shift) % drawn.shape[longest]
        spots.append(tuple(where))
    return drawn.at[spots[0]].set(least).at[spots[1]].set(largest)


def levels(key, shape, cuts, smallest, high):
    level = 1.0
    for dim, blocks in cuts:
        draws = jax.random.uniform(jax.random.fold_in(jax.random.fold_in(key, 6), dim), (blocks,), jnp.float32, smallest / len(cuts), high / len(cuts))
        level = level * jnp.repeat(jnp.exp(draws), shape[dim] // blocks).reshape((-1,) + (1,) * (len(shape) - 1 - dim))
    return level


def cumulative_ranks(amount, slope):
    loads = [(1 << 20) // math.isqrt(grade ** slope) + 1 for grade in range(1, amount + 1)]
    width = 1 + sum(loads) // (1 << 30)
    return np.cumsum(np.array([max(1, weight // width) for weight in loads]))


def ranked(stream_key, dims, number_of, lean):
    grid = cumulative_ranks(number_of, lean)
    ticket = jax.random.randint(jax.random.fold_in(stream_key, 1), dims, 0, int(grid[number_of - 1]))
    grade = jnp.searchsorted(jnp.asarray(grid, jnp.int32), ticket, side="right")
    return jax.random.permutation(jax.random.fold_in(stream_key, 2), number_of)[grade].astype(jnp.int32)


def centred(stream_key, extent, width, bound, cuts=(), kind=jnp.bfloat16):
    array = width * jax.random.normal(stream_key, extent, jnp.float32)
    if cuts:
        array = array * levels(stream_key, extent, cuts, -0.22, 0.18)
    return jnp.clip(array, -bound, bound).astype(kind)


def setup_inputs(seed: int = 0) -> dict:
    seeds = jax.random.split(jax.random.key(seed), 12)
    return {
        "query_in": draw_query_in(jax.random.fold_in(seeds[11], 71), 0),
        "key_in": draw_key_in(jax.random.fold_in(seeds[11], 71), 0),
        "value_in": centred(seeds[2], (HOLDERS, BATCHES, RESP_LEN, KVW), 1.0, 6.0, ((0, 8), (1, 128))),
        "prefix_key": centred(seeds[3], (HOLDERS, BATCHES, PLEN, KVW), 1.0, 6.0, ((0, 8), (1, 128))),
        "prefix_value": centred(seeds[4], (HOLDERS, BATCHES, PLEN, KVW), 1.0, 6.0, ((0, 8), (1, 128))),
        "q_bias": draw_q_bias(jax.random.fold_in(seeds[11], 71), 0),
        "out_grad": centred(seeds[6], (HOLDERS, BATCHES, RESP_LEN, QW), 1.0, 6.0, ((0, 8), (1, 128))),
        "group": touch_ends(ranked(seeds[7], (HOLDERS, BATCHES), HOLDERS, 2), jax.random.fold_in(seeds[7], 3), 0, HOLDERS - 1).astype(jnp.int32),
        "resp_len": touch_ends(jax.random.randint(seeds[8], (HOLDERS, BATCHES), 1, RESP_LEN + 1), jax.random.fold_in(seeds[8], 1), 1, RESP_LEN).astype(jnp.int32),
        "pref_blocks": touch_ends(jax.random.randint(seeds[9], (HOLDERS, BATCHES), 1, PREF_BLOCKS + 1), jax.random.fold_in(seeds[9], 1), 1, PREF_BLOCKS).astype(jnp.int32),
        "keep": touch_ends((jax.random.randint(seeds[10], (HOLDERS, BATCHES, PREF_BLOCKS), 0, 4) < 3).astype(jnp.int32), jax.random.fold_in(seeds[10], 1), 0, 1),
    }


masked_score = -1.0e30


def attend_grads(query_biased, prefix_keys, prefix_vals, self_keys, self_vals, grad_rows, prefix_mask):
    row_count = query_biased.shape[0]
    prefix_len = prefix_keys.shape[0]
    kv_heads = prefix_keys.shape[1] // HEAD_DIM
    group_size = query_biased.shape[1] // prefix_keys.shape[1]
    score_scale = HEAD_DIM ** -0.5
    queries = query_biased.astype(jnp.float32).reshape(row_count, kv_heads, group_size, HEAD_DIM)
    key_rows = jnp.concatenate([prefix_keys, self_keys], axis=0).astype(jnp.float32).reshape(prefix_len + row_count, kv_heads, HEAD_DIM)
    val_rows = jnp.concatenate([prefix_vals, self_vals], axis=0).astype(jnp.float32).reshape(prefix_len + row_count, kv_heads, HEAD_DIM)
    cotangent = grad_rows.astype(jnp.float32).reshape(row_count, kv_heads, group_size, HEAD_DIM)
    scores = jnp.einsum("tkgd,skd->kgts", queries, key_rows) * score_scale
    positions = jnp.arange(row_count, dtype=jnp.int32)
    causal = positions[None, :] <= positions[:, None]
    allowed = jnp.concatenate([jnp.broadcast_to(prefix_mask[None, :], (row_count, prefix_len)), causal], axis=1)
    scores = jnp.where(allowed, scores, masked_score)
    row_peak = jnp.max(scores, axis=-1, keepdims=True)
    expon = jnp.exp(scores - row_peak)
    probs = expon / jnp.sum(expon, axis=-1, keepdims=True)
    probs_low = lax.optimization_barrier(probs.astype(jnp.bfloat16)).astype(jnp.float32)
    attended = jnp.einsum("kgts,skd->tkgd", probs_low, val_rows)
    dprobs = jnp.einsum("tkgd,skd->kgts", cotangent, val_rows)
    row_delta = jnp.transpose(jnp.sum(cotangent * attended, axis=-1), (1, 2, 0))[..., None]
    dscores = probs * (dprobs - row_delta)
    dscores_low = lax.optimization_barrier(dscores.astype(jnp.bfloat16)).astype(jnp.float32)
    q_full = jnp.einsum("kgts,skd->tkgd", dscores_low, key_rows).reshape(row_count, -1) * score_scale
    key_part = jnp.einsum("kgts,tkgd->skd", dscores_low, queries).reshape(prefix_len + row_count, -1) * score_scale
    value_part = jnp.einsum("kgts,tkgd->skd", probs_low, cotangent).reshape(prefix_len + row_count, -1)
    return q_full, key_part, value_part


def reference(query_in, key_in, value_in, prefix_key, prefix_value, q_bias, out_grad, group, resp_len, pref_blocks, keep):
    def one_response(number):
        resp_idx = number // BATCHES
        batch_idx = number % BATCHES
        holder = group[resp_idx, batch_idx]
        query_biased = (query_in[resp_idx, batch_idx].astype(jnp.float32) + q_bias.astype(jnp.float32)).astype(jnp.bfloat16)
        block_ids = jnp.arange(PLEN, dtype=jnp.int32) // BLOCK
        kept = jnp.repeat(keep[resp_idx, batch_idx], BLOCK, total_repeat_length=PLEN)
        prefix_mask = (block_ids < pref_blocks[holder, batch_idx]) & (kept == 1)
        live_rows = jnp.arange(RESP_LEN, dtype=jnp.int32) < resp_len[resp_idx, batch_idx]
        grad_rows = jnp.where(live_rows[:, None], out_grad[resp_idx, batch_idx], jnp.zeros((), jnp.bfloat16))
        q_full, key_part, value_part = attend_grads(query_biased, prefix_key[holder, batch_idx], prefix_value[holder, batch_idx], key_in[resp_idx, batch_idx], value_in[resp_idx, batch_idx], grad_rows, prefix_mask)
        return (q_full.astype(jnp.bfloat16), key_part[PLEN:].astype(jnp.bfloat16), value_part[PLEN:].astype(jnp.bfloat16), key_part[:PLEN].astype(jnp.bfloat16), value_part[:PLEN].astype(jnp.bfloat16), jnp.sum(q_full, axis=0), jnp.sum(value_part, axis=0))

    results = lax.map(one_response, jnp.arange(HOLDERS * BATCHES, dtype=jnp.int32))
    q_grad = results[0].reshape(HOLDERS, BATCHES, RESP_LEN, QW)
    key_grad = results[1].reshape(HOLDERS, BATCHES, RESP_LEN, KVW)
    value_grad = results[2].reshape(HOLDERS, BATCHES, RESP_LEN, KVW)
    segment_ids = (group * BATCHES + jnp.arange(BATCHES, dtype=jnp.int32)[None, :]).reshape(-1)
    prefix_key_grad = jax.ops.segment_sum(results[3].astype(jnp.float32), segment_ids, num_segments=HOLDERS * BATCHES).astype(jnp.bfloat16).reshape(HOLDERS, BATCHES, PLEN, KVW)
    prefix_value_grad = jax.ops.segment_sum(results[4].astype(jnp.float32), segment_ids, num_segments=HOLDERS * BATCHES).astype(jnp.bfloat16).reshape(HOLDERS, BATCHES, PLEN, KVW)
    devices_count = HOLDERS * BATCHES
    q_bias_grad = jnp.sum(results[5], axis=0) / devices_count
    v_bias_grad = jnp.sum(results[6], axis=0) / devices_count
    return (q_grad, key_grad, value_grad, prefix_key_grad, prefix_value_grad, q_bias_grad, v_bias_grad)
```

```python
import functools

import jax
import jax.numpy as jnp
from jax import lax
from jax.experimental import pallas as pl
from jax.experimental.pallas import tpu as pltpu
from jax.sharding import Mesh
from jax.sharding import PartitionSpec as P

HD = 128
ROWS = 128
KVH = 4
GRP = 5
QH = GRP * HD
CHIPS = 4
DP = ("dp_0", "dp_1")
NEG = -1e30
SCALE = HD ** (-0.5)
LOG2E = 1.4426950408889634
F32 = jnp.float32
BF16 = jnp.bfloat16
NT = (((1,), (1,)), ((), ()))
NN = (((1,), (0,)), ((), ()))
TN = (((0,), (0,)), ((), ()))


def dot(a, b, dims):
    return lax.dot_general(a, b, dims, preferred_element_type=F32)


def place():
    r = lax.axis_index("resp")
    y, core = r // 2, lax.rem(r, 2)
    left = lax.rem(y + CHIPS - 1, CHIPS)
    right = lax.rem(y + 1, CHIPS)
    return r, y, core, left, right


def remote(src, dst, send, recv, resp):
    return pltpu.make_async_remote_copy(
        src_ref=src, dst_ref=dst, send_sem=send, recv_sem=recv,
        device_id={"resp": resp}, device_id_type=pl.DeviceIdType.MESH)


def greet(r):
    barrier = pltpu.get_barrier_semaphore()
    for o in range(1, 8):
        pl.semaphore_signal(barrier, inc=1, device_id={"resp": lax.rem(r + o, 8)},
                            device_id_type=pl.DeviceIdType.MESH)
    pl.semaphore_wait(barrier, 7)


def attend_kernel(group, resp_len, blocks, keep, query, keys, vals, pk, pv, bias, grad,
                  dq_out, dk_out, dv_out, part_out, share, meta,
                  own, mate, r1r, r1l, x1r, x1l, s2l, s2r, r2l, r2r,
                  qv, gv, kv, vv, qs, gs, ss, dps, st, dpt, kf, vf, pb, ds, dqv, dkv, dvv, part,
                  in_sem, pre_sem, out_sem, msend, mrecv, csend, crecv):
    r, y, core, left, right = place()
    mate_id = y * 2 + 1 - core
    left_id = left * 2 + core
    right_id = right * 2 + core

    pre = []
    for h in range(KVH):
        col = pl.ds(h * HD, HD)
        pre.append(pltpu.make_async_copy(pk.at[0, 0, :, col], own.at[h, 0], pre_sem.at[h, 0]))
        pre.append(pltpu.make_async_copy(pv.at[0, 0, :, col], own.at[h, 1], pre_sem.at[h, 1]))
    for c in pre:
        c.start()
    loads = [pltpu.make_async_copy(a.at[0, 0], b, in_sem.at[i])
             for i, (a, b) in enumerate(((query, qv), (grad, gv), (keys, kv), (vals, vv)))]
    for c in loads:
        c.start()
    my_group = group[0, 0]
    meta[pl.ds(r, 1)] = jnp.full((1, 8, HD), my_group * 4 + blocks[0, 0], jnp.int32)
    greet(r)

    notes = [remote(meta.at[r], meta.at[r], msend.at[o - 1], mrecv.at[o - 1], lax.rem(r + o, 8))
             for o in range(1, 8)]
    for c in notes:
        c.start()

    def lo(ref, h):
        return ref.at[h, :, pl.ds(0, 128), :]

    def hi(ref, h):
        return ref.at[h, :, pl.ds(128, 128), :]

    def first(h):
        return (remote(own.at[h], mate.at[h], csend.at[0, h], crecv.at[0, h], mate_id),
                remote(lo(own, h), r1r.at[h], csend.at[1, h], crecv.at[1, h], left_id),
                remote(hi(own, h), r1l.at[h], csend.at[2, h], crecv.at[2, h], right_id))

    def shared(h):
        return (remote(r1r.at[h], x1r.at[h], csend.at[3, h], crecv.at[3, h], mate_id),
                remote(r1l.at[h], x1l.at[h], csend.at[4, h], crecv.at[4, h], mate_id))

    def second(h):
        return (remote(s2l.at[h], r2r.at[h], csend.at[5, h], crecv.at[5, h], left_id),
                remote(s2r.at[h], r2l.at[h], csend.at[6, h], crecv.at[6, h], right_id))

    for h in range(KVH):
        pre[2 * h].wait()
        pre[2 * h + 1].wait()
        for c in first(h):
            c.start()
    for c in loads:
        c.wait()
    for c in notes:
        c.wait_recv()

    info = [jnp.max(meta[i]) for i in range(8)]
    holder_blocks = jnp.int32(0)
    for i in range(8):
        holder_blocks = jnp.where(my_group == i, lax.rem(info[i], 4), holder_blocks)

    def of(idx):
        word = jnp.int32(0)
        for i in range(8):
            word = jnp.where(idx == i, info[i], word)
        g = word // 4
        return lax.rem(g // 2 - y + CHIPS, CHIPS), lax.rem(g, 2) == core

    rel_l, same_l = of(left_id)
    rel_r, same_r = of(right_id)
    rel, same = of(r)
    ok0 = keep[0, 0, 0] == 1
    ok1 = jnp.logical_and(holder_blocks > 1, keep[0, 0, 1] == 1)
    live = lax.broadcasted_iota(jnp.int32, (ROWS, HD), 0) < resp_len[0, 0]
    causal = (lax.broadcasted_iota(jnp.int32, (ROWS, ROWS), 0)
              <= lax.broadcasted_iota(jnp.int32, (ROWS, ROWS), 1))

    def prework(h, carry):
        for c in shared_start(h):
            c.start()
        for g in range(GRP):
            col = pl.ds(pl.multiple_of(h * QH + g * HD, HD), HD)
            rows = pl.ds(g * ROWS, ROWS)
            q = qv[:, col].astype(F32) + bias[:, col].astype(F32)
            qs[h, rows, :] = q.astype(BF16)
            gs[h, rows, :] = jnp.where(live, gv[:, col].astype(F32), 0.0).astype(BF16)
        kcol = pl.ds(pl.multiple_of(h * HD, HD), HD)
        s = dot(kv[:, kcol], qs[h], NT) * (SCALE * LOG2E)
        for g in range(GRP):
            ss[h, :, g * ROWS:(g + 1) * ROWS] = jnp.where(
                causal, s[:, g * ROWS:(g + 1) * ROWS], NEG)
        dps[h] = dot(vv[:, kcol], gs[h], NT)
        mine, r1a, r1b = first(h)
        mine.wait_recv()
        for c in shared(h):
            c.wait_recv()
        mine_l = jnp.where(same_l, own[h, :, 128:256, :], mate[h, :, 128:256, :])
        far_l = jnp.where(same_l, r1r[h], x1r[h])
        s2l[h] = jnp.where(rel_l == 0, mine_l, far_l)
        mine_r = jnp.where(same_r, own[h, :, 0:128, :], mate[h, :, 0:128, :])
        far_r = jnp.where(same_r, r1l[h], x1l[h])
        s2r[h] = jnp.where(rel_r == 0, mine_r, far_r)
        for c in second(h):
            c.start()
        return carry

    def shared_start(h):
        _, a, b = first(h)
        a.wait_recv()
        b.wait_recv()
        return shared(h)

    lax.fori_loop(0, KVH, prework, 0)

    def main(h, carry):
        for c in second(h):
            c.wait_recv()
        kcol = pl.ds(pl.multiple_of(h * HD, HD), HD)
        near = jnp.where(same, own[h, :, 0:128, :], mate[h, :, 0:128, :])
        step1 = jnp.where(same, r1r[h], x1r[h])
        low = jnp.where(rel == 0, near, jnp.where(rel == 1, step1, jnp.where(rel == 3, r2l[h], r2r[h])))
        near = jnp.where(same, own[h, :, 128:256, :], mate[h, :, 128:256, :])
        step1 = jnp.where(same, r1l[h], x1l[h])
        high = jnp.where(rel == 0, near, jnp.where(rel == 3, step1, jnp.where(rel == 1, r2r[h], r2l[h])))
        kf[0:128] = low[0]
        kf[128:256] = high[0]
        kf[256:384] = kv[:, kcol]
        vf[0:128] = low[1]
        vf[128:256] = high[1]
        st[...] = dot(kf[0:256], qs[h], NT)
        dpt[...] = dot(vf[0:256], gs[h], NT)
        for g in range(GRP):
            c = pl.ds(g * ROWS, ROWS)
            s0 = jnp.where(ok0, st[0:128, c] * (SCALE * LOG2E), NEG)
            s1 = jnp.where(ok1, st[128:256, c] * (SCALE * LOG2E), NEG)
            s2 = ss[h, :, c]
            peak = jnp.max(jnp.maximum(jnp.maximum(s0, s1), s2), axis=0, keepdims=True)
            e0, e1, e2 = jnp.exp2(s0 - peak), jnp.exp2(s1 - peak), jnp.exp2(s2 - peak)
            inv = 1.0 / jnp.sum(e0 + e1 + e2, axis=0, keepdims=True)
            p0, p1, p2 = e0 * inv, e1 * inv, e2 * inv
            b0, b1, b2 = p0.astype(BF16), p1.astype(BF16), p2.astype(BF16)
            pb[0:128, c] = b0
            pb[128:256, c] = b1
            pb[256:384, c] = b2
            d0, d1, d2 = dpt[0:128, c], dpt[128:256, c], dps[h, :, c]
            delta = jnp.sum(b0.astype(F32) * d0 + b1.astype(F32) * d1 + b2.astype(F32) * d2,
                            axis=0, keepdims=True)
            ds[0:128, c] = (p0 * (d0 - delta)).astype(BF16)
            ds[128:256, c] = (p1 * (d1 - delta)).astype(BF16)
            ds[256:384, c] = (p2 * (d2 - delta)).astype(BF16)
        dv = dot(pb[...], gs[h], NN)
        share[:, pl.ds(pl.multiple_of(KVH * QH + h * HD, HD), HD)] = jnp.sum(dv, axis=0, keepdims=True)
        part[h, 1] = dv[0:256].astype(BF16)
        dvv[:, kcol] = dv[256:384].astype(BF16)
        dk = dot(ds[...], qs[h], NN) * SCALE
        part[h, 0] = dk[0:256].astype(BF16)
        dkv[:, kcol] = dk[256:384].astype(BF16)
        dq = dot(ds[...], kf[...], TN) * SCALE
        for g in range(GRP):
            col = pl.ds(pl.multiple_of(h * QH + g * HD, HD), HD)
            one = dq[g * ROWS:(g + 1) * ROWS]
            share[:, col] = jnp.sum(one, axis=0, keepdims=True)
            dqv[:, col] = one.astype(BF16)
        put(h)[0].start()
        put(h)[1].start()
        return carry

    def put(h):
        col = pl.ds(pl.multiple_of(h * QH, HD), QH)
        return (pltpu.make_async_copy(dqv.at[:, col], dq_out.at[0, 0, :, col], out_sem.at[h]),
                pltpu.make_async_copy(part.at[h], part_out.at[h], out_sem.at[KVH + h]))

    kf[256:384] = kv[:, 0:HD]
    lax.fori_loop(0, KVH, main, 0)
    last = (pltpu.make_async_copy(dkv, dk_out.at[0, 0], out_sem.at[2 * KVH]),
            pltpu.make_async_copy(dvv, dv_out.at[0, 0], out_sem.at[2 * KVH + 1]))
    for c in last:
        c.start()
    for c in notes:
        c.wait_send()
    for h in range(KVH):
        for c in (*first(h), *shared(h), *second(h)):
            c.wait_send()
        for c in put(h):
            c.wait()
    for c in last:
        c.wait()


def vmem(*shape, dtype=BF16):
    return pltpu.VMEM(shape, dtype)


def attend(group, resp_len, blocks, keep, query, keys, vals, pk, pv, bias, grad):
    smem = pl.BlockSpec(memory_space=pltpu.SMEM)
    anywhere = pl.BlockSpec(memory_space=pl.ANY)
    inside = pl.BlockSpec(memory_space=pltpu.VMEM)
    half = vmem(KVH, 2, 128, HD)
    out = jax.ShapeDtypeStruct
    return pl.pallas_call(
        attend_kernel,
        out_shape=(out(query.shape, BF16), out(keys.shape, BF16), out(vals.shape, BF16),
                   out((KVH, 2, 256, HD), BF16), out((1, KVH * QH + KVH * HD), F32),
                   out((8, 8, HD), jnp.int32)),
        in_specs=[smem] * 4 + [anywhere] * 5 + [inside] + [anywhere],
        out_specs=(anywhere,) * 4 + (inside, inside),
        scratch_shapes=[
            vmem(KVH, 2, 256, HD), vmem(KVH, 2, 256, HD),
            half, half, half, half, half, half, half, half,
            vmem(ROWS, KVH * QH), vmem(ROWS, KVH * QH), vmem(ROWS, KVH * HD), vmem(ROWS, KVH * HD),
            vmem(KVH, QH, HD), vmem(KVH, QH, HD),
            vmem(KVH, ROWS, QH, dtype=F32), vmem(KVH, ROWS, QH, dtype=F32),
            vmem(256, QH, dtype=F32), vmem(256, QH, dtype=F32),
            vmem(384, HD), vmem(256, HD), vmem(384, QH), vmem(384, QH),
            vmem(ROWS, KVH * QH), vmem(ROWS, KVH * HD), vmem(ROWS, KVH * HD), vmem(KVH, 2, 256, HD),
            pltpu.SemaphoreType.DMA((4,)), pltpu.SemaphoreType.DMA((KVH, 2)),
            pltpu.SemaphoreType.DMA((2 * KVH + 2,)),
            pltpu.SemaphoreType.DMA((7,)), pltpu.SemaphoreType.DMA((7,)),
            pltpu.SemaphoreType.DMA((7, KVH)), pltpu.SemaphoreType.DMA((7, KVH)),
        ],
        compiler_params=pltpu.CompilerParams(collective_id=0, has_side_effects=True),
        name="attend",
    )(group, resp_len, blocks, keep, query, keys, vals, pk, pv, bias, grad)


def settle_kernel(meta, part, pkg_out, pvg_out,
                  mine, sl, sr, mate, zr, zl, xr, xl, fr, fl, gl, gr, kg, vg,
                  in_sem, out_sem, csend, crecv):
    r, y, core, left, right = place()
    mate_id = y * 2 + 1 - core
    left_id = left * 2 + core
    right_id = right * 2 + core
    loads = [pltpu.make_async_copy(part.at[h], mine.at[h], in_sem.at[h]) for h in range(KVH)]
    for c in loads:
        c.start()

    def of(idx):
        g = jnp.max(meta[idx]) // 4
        return lax.rem(g // 2 - y + CHIPS, CHIPS), lax.rem(g, 2) == core

    rel, same = of(r)
    rel_m, same_m = of(mate_id)
    from_r = (of(right_id), of(right * 2 + 1 - core))
    from_l = (of(left_id), of(left * 2 + 1 - core))
    greet(r)

    def first(h):
        return (remote(mine.at[h], mate.at[h], csend.at[0, h], crecv.at[0, h], mate_id),
                remote(sl.at[h], zr.at[h], csend.at[1, h], crecv.at[1, h], left_id),
                remote(sr.at[h], zl.at[h], csend.at[2, h], crecv.at[2, h], right_id))

    def shared(h):
        return (remote(zr.at[h], xr.at[h], csend.at[3, h], crecv.at[3, h], mate_id),
                remote(zl.at[h], xl.at[h], csend.at[4, h], crecv.at[4, h], mate_id))

    def second(h):
        return (remote(fr.at[h], gl.at[h], csend.at[5, h], crecv.at[5, h], right_id),
                remote(fl.at[h], gr.at[h], csend.at[6, h], crecv.at[6, h], left_id))

    for h in range(KVH):
        loads[h].wait()
        sl[h] = jnp.where(rel == 3, mine[h, :, 0:128, :], mine[h, :, 128:256, :])
        sr[h] = jnp.where(rel == 1, mine[h, :, 128:256, :], mine[h, :, 0:128, :])
    for h in range(KVH):
        for c in first(h):
            c.start()

    def total(terms):
        out = 0.0
        for hit, x in terms:
            out = out + jnp.where(hit, x.astype(F32), 0.0)
        return out

    def both(a, b):
        return jnp.logical_and(a, b)

    def pass_on(h, carry):
        keep_m, a, b = first(h)
        a.wait_recv()
        b.wait_recv()
        for c in shared(h):
            c.start()
        keep_m.wait_recv()
        for c in shared(h):
            c.wait_recv()
        fr[h] = total(((both(rel == 1, same), mine[h, :, 0:128, :]),
                       (both(rel_m == 1, same_m), mate[h, :, 0:128, :]),
                       (both(from_l[0][0] == 1, from_l[0][1]), zl[h]),
                       (both(from_l[1][0] == 1, from_l[1][1]), xl[h]))).astype(BF16)
        fl[h] = total(((both(rel == 3, same), mine[h, :, 128:256, :]),
                       (both(rel_m == 3, same_m), mate[h, :, 128:256, :]),
                       (both(from_r[0][0] == 3, from_r[0][1]), zr[h]),
                       (both(from_r[1][0] == 3, from_r[1][1]), xr[h]))).astype(BF16)
        for c in second(h):
            c.start()
        return carry

    lax.fori_loop(0, KVH, pass_on, 0)

    def finish(h, carry):
        for c in second(h):
            c.wait_recv()
        col = pl.ds(pl.multiple_of(h * HD, HD), HD)
        low = total(((both(rel == 0, same), mine[h, :, 0:128, :]),
                     (both(rel_m == 0, same_m), mate[h, :, 0:128, :]),
                     (both(from_r[0][0] == 0, from_r[0][1]), zr[h]),
                     (both(from_r[1][0] == 0, from_r[1][1]), xr[h]))) + gl[h].astype(F32)
        high = total(((both(rel == 0, same), mine[h, :, 128:256, :]),
                      (both(rel_m == 0, same_m), mate[h, :, 128:256, :]),
                      (both(from_l[0][0] == 0, from_l[0][1]), zl[h]),
                      (both(from_l[1][0] == 0, from_l[1][1]), xl[h]))) + gr[h].astype(F32)
        kg[0:128, col] = low[0].astype(BF16)
        kg[128:256, col] = high[0].astype(BF16)
        vg[0:128, col] = low[1].astype(BF16)
        vg[128:256, col] = high[1].astype(BF16)
        return carry

    lax.fori_loop(0, KVH, finish, 0)
    outs = (pltpu.make_async_copy(kg, pkg_out.at[0, 0], out_sem.at[0]),
            pltpu.make_async_copy(vg, pvg_out.at[0, 0], out_sem.at[1]))
    for c in outs:
        c.start()
    for h in range(KVH):
        for c in (*first(h), *shared(h), *second(h)):
            c.wait_send()
    for c in outs:
        c.wait()


def settle(meta, part):
    anywhere = pl.BlockSpec(memory_space=pl.ANY)
    half = vmem(KVH, 2, 128, HD)
    whole = vmem(KVH, 2, 256, HD)
    grad = jax.ShapeDtypeStruct((1, 1, 256, KVH * HD), BF16)
    return pl.pallas_call(
        settle_kernel,
        out_shape=(grad, grad),
        in_specs=[pl.BlockSpec(memory_space=pltpu.VMEM), anywhere],
        out_specs=(anywhere, anywhere),
        scratch_shapes=[
            whole, half, half, whole, half, half, half, half, half, half, half, half,
            vmem(256, KVH * HD), vmem(256, KVH * HD),
            pltpu.SemaphoreType.DMA((KVH,)), pltpu.SemaphoreType.DMA((2,)),
            pltpu.SemaphoreType.DMA((7, KVH)), pltpu.SemaphoreType.DMA((7, KVH)),
        ],
        compiler_params=pltpu.CompilerParams(collective_id=1, has_side_effects=True),
        name="settle",
        cost_estimate=pl.CostEstimate(flops=10**7, bytes_accessed=4 * 10**7, transcendentals=0),
    )(meta, part)


def per_device(query_in, key_in, value_in, prefix_key, prefix_value, q_bias, out_grad,
               group, resp_len, pref_blocks, keep):
    dq, dk, dv, part, share, meta = attend(
        group, resp_len, pref_blocks, keep, query_in, key_in, value_in,
        prefix_key, prefix_value, q_bias.reshape(1, -1), out_grad)
    plane = ("resp", "dp_0")
    members = lax.axis_size(plane)
    line = lax.axis_size("dp_1")
    width = share.shape[1]
    pieces = lax.all_to_all(share.reshape(members, width // members), plane, 0, 0, tiled=True)
    piece = jnp.sum(pieces, axis=0)
    rows = lax.all_to_all(jnp.broadcast_to(piece[None], (line, piece.shape[0])), "dp_1", 0, 0, tiled=True)
    pkg, pvg = settle(meta, part)
    piece = jnp.sum(rows, axis=0) / (lax.axis_size("resp") * lax.axis_size(DP))
    whole = lax.all_to_all(jnp.broadcast_to(piece[None], (members, piece.shape[0])), plane, 0, 0, tiled=True)
    whole = whole.reshape(width)
    return dq, dk, dv, pkg, pvg, whole[:KVH * QH], whole[KVH * QH:]


def solution(mesh):
    split = Mesh(mesh.devices.reshape(mesh.shape["resp"], 4, mesh.shape["dp"] // 4), ("resp", *DP))
    rows = P("resp", DP, None, None)
    in_specs = (rows, rows, rows, rows, rows, P(), rows,
                P("resp", DP), P("resp", DP), P("resp", DP), P("resp", DP, None))
    return jax.shard_map(per_device, mesh=split, in_specs=in_specs,
                         out_specs=(rows,) * 5 + (P(), P()), check_vma=False)
```

```python
import functools

import jax
import jax.numpy as jnp
from jax import lax
from jax.experimental import pallas as pl
from jax.experimental.pallas import tpu as pltpu
from jax.sharding import Mesh
from jax.sharding import PartitionSpec as P

HD = 128
ROWS = 128
KVH = 4
GRP = 5
QH = GRP * HD
CHIPS = 4
DP = ("dp_0", "dp_1")
NEG = -1e30
SCALE = HD ** (-0.5)
LOG2E = 1.4426950408889634
F32 = jnp.float32
BF16 = jnp.bfloat16
NT = (((1,), (1,)), ((), ()))
NN = (((1,), (0,)), ((), ()))
TN = (((0,), (0,)), ((), ()))


def dot(a, b, dims):
    return lax.dot_general(a, b, dims, preferred_element_type=F32)


def place():
    r = lax.axis_index("resp")
    y, core = r // 2, lax.rem(r, 2)
    left = lax.rem(y + CHIPS - 1, CHIPS)
    right = lax.rem(y + 1, CHIPS)
    return r, y, core, left, right


def remote(src, dst, send, recv, target, axis="resp"):
    return pltpu.make_async_remote_copy(
        src_ref=src, dst_ref=dst, send_sem=send, recv_sem=recv,
        device_id={axis: target}, device_id_type=pl.DeviceIdType.MESH)


def tell(sem, target, axis="resp"):
    pl.semaphore_signal(sem, inc=1, device_id={axis: target}, device_id_type=pl.DeviceIdType.MESH)


def total(terms):
    out = 0.0
    for hit, x in terms:
        out = out + jnp.where(hit, x.astype(F32), 0.0)
    return out


def kernel(xs, zs, group, resp_len, blocks, keep, query, keys, vals, pk, pv, bias, grad,
           dq_out, dk_out, dv_out, pkg_out, pvg_out, sums,
           meta, own, mate, r1r, r1l, x1r, x1l, s2l, s2r, r2l, r2r,
           qv, gv, kv, vv, qs, gs, ss, dps, st, dpt, kf, vf, pb, ds, dqv, dkv, dvv, part,
           pmate, sl, sr, zr, zl, xr, xl, fr, fl, gl, gr, kg, vg,
           share, b1, row, b2, zrow, zall, piece,
           in_sem, pre_sem, out_sem, msend, mrecv, csend, crecv, ssend, srecv,
           b1s, b1r, b2s, b2r, b3s, b3r, b4s, b4r, b5s, b5r, near_sem):
    r, y, core, left, right = place()
    xi, zi = lax.axis_index("dp_0"), lax.axis_index("dp_1")
    mate_id = y * 2 + 1 - core
    left_id = left * 2 + core
    right_id = right * 2 + core
    rounds = max(zs.bit_length() - 2, 0)

    pre = []
    for h in range(KVH):
        col = pl.ds(h * HD, HD)
        pre.append(pltpu.make_async_copy(pk.at[0, 0, :, col], own.at[h, 0], pre_sem.at[h, 0]))
        pre.append(pltpu.make_async_copy(pv.at[0, 0, :, col], own.at[h, 1], pre_sem.at[h, 1]))
    for c in pre:
        c.start()
    loads = [pltpu.make_async_copy(a.at[0, 0], b, in_sem.at[i])
             for i, (a, b) in enumerate(((query, qv), (grad, gv), (keys, kv), (vals, vv)))]
    for c in loads:
        c.start()
    my_group = group[0, 0]
    meta[pl.ds(r, 1)] = jnp.full((1, 8, HD), my_group * 4 + blocks[0, 0], jnp.int32)
    share[...] = jnp.zeros_like(share)

    barrier = pltpu.get_barrier_semaphore()
    for o in range(1, 8):
        tell(barrier, lax.rem(r + o, 8))
    for o in range(1, xs):
        tell(barrier, lax.rem(xi + o, xs), "dp_0")
    if zs > 1:
        tell(barrier, lax.rem(zi + 1, zs), "dp_1")
        tell(barrier, lax.rem(zi + zs - 1, zs), "dp_1")
    pl.semaphore_wait(barrier, 7 + xs - 1 + (2 if zs > 1 else 0))

    notes = [remote(meta.at[r], meta.at[r], msend.at[o - 1], mrecv.at[o - 1], lax.rem(r + o, 8))
             for o in range(1, 8)]
    for c in notes:
        c.start()

    def lo(ref, h):
        return ref.at[h, :, pl.ds(0, 128), :]

    def hi(ref, h):
        return ref.at[h, :, pl.ds(128, 128), :]

    def first(h):
        return (remote(own.at[h], mate.at[h], csend.at[0, h], crecv.at[0, h], mate_id),
                remote(lo(own, h), r1r.at[h], csend.at[1, h], crecv.at[1, h], left_id),
                remote(hi(own, h), r1l.at[h], csend.at[2, h], crecv.at[2, h], right_id))

    def shared(h):
        return (remote(r1r.at[h], x1r.at[h], csend.at[3, h], crecv.at[3, h], mate_id),
                remote(r1l.at[h], x1l.at[h], csend.at[4, h], crecv.at[4, h], mate_id))

    def second(h):
        return (remote(s2l.at[h], r2r.at[h], csend.at[5, h], crecv.at[5, h], left_id),
                remote(s2r.at[h], r2l.at[h], csend.at[6, h], crecv.at[6, h], right_id))

    def back_first(h):
        return (remote(part.at[h], pmate.at[h], ssend.at[0, h], srecv.at[0, h], mate_id),
                remote(sl.at[h], zr.at[h], ssend.at[1, h], srecv.at[1, h], left_id),
                remote(sr.at[h], zl.at[h], ssend.at[2, h], srecv.at[2, h], right_id))

    def back_shared(h):
        return (remote(zr.at[h], xr.at[h], ssend.at[3, h], srecv.at[3, h], mate_id),
                remote(zl.at[h], xl.at[h], ssend.at[4, h], srecv.at[4, h], mate_id))

    def back_second(h):
        return (remote(fr.at[h], gl.at[h], ssend.at[5, h], srecv.at[5, h], right_id),
                remote(fl.at[h], gr.at[h], ssend.at[6, h], srecv.at[6, h], left_id))

    for h in range(KVH):
        pre[2 * h].wait()
        pre[2 * h + 1].wait()
        for c in first(h):
            c.start()
    for c in loads:
        c.wait()
    for c in notes:
        c.wait_recv()

    info = [jnp.max(meta[i]) for i in range(8)]

    def look(idx):
        word = jnp.int32(0)
        for i in range(8):
            word = jnp.where(idx == i, info[i], word)
        return word

    def of(idx):
        g = look(idx) // 4
        return lax.rem(g // 2 - y + CHIPS, CHIPS), lax.rem(g, 2) == core

    holder_blocks = lax.rem(look(my_group), 4)
    rel, same = of(r)
    rel_m, same_m = of(mate_id)
    rel_l, same_l = of(left_id)
    rel_r, same_r = of(right_id)
    rel_lx, same_lx = of(left * 2 + 1 - core)
    rel_rx, same_rx = of(right * 2 + 1 - core)
    ok0 = keep[0, 0, 0] == 1
    ok1 = jnp.logical_and(holder_blocks > 1, keep[0, 0, 1] == 1)
    live = lax.broadcasted_iota(jnp.int32, (ROWS, HD), 0) < resp_len[0, 0]
    causal = (lax.broadcasted_iota(jnp.int32, (ROWS, ROWS), 0)
              <= lax.broadcasted_iota(jnp.int32, (ROWS, ROWS), 1))

    def prework(h, reach):
        if rounds == KVH:
            tell(near_sem.at[h, 0], lax.rem(zi + reach, zs), "dp_1")
            tell(near_sem.at[h, 1], lax.rem(zi + zs - reach, zs), "dp_1")
        _, a, b = first(h)
        a.wait_recv()
        b.wait_recv()
        for c in shared(h):
            c.start()
        for g in range(GRP):
            col = pl.ds(pl.multiple_of(h * QH + g * HD, HD), HD)
            rows = pl.ds(g * ROWS, ROWS)
            q = qv[:, col].astype(F32) + bias[:, col].astype(F32)
            qs[h, rows, :] = q.astype(BF16)
            gs[h, rows, :] = jnp.where(live, gv[:, col].astype(F32), 0.0).astype(BF16)
        kcol = pl.ds(pl.multiple_of(h * HD, HD), HD)
        s = dot(kv[:, kcol], qs[h], NT) * (SCALE * LOG2E)
        for g in range(GRP):
            ss[h, :, g * ROWS:(g + 1) * ROWS] = jnp.where(
                causal, s[:, g * ROWS:(g + 1) * ROWS], NEG)
        dps[h] = dot(vv[:, kcol], gs[h], NT)
        first(h)[0].wait_recv()
        for c in shared(h):
            c.wait_recv()
        mine_l = jnp.where(same_l, own[h, :, 128:256, :], mate[h, :, 128:256, :])
        far_l = jnp.where(same_l, r1r[h], x1r[h])
        s2l[h] = jnp.where(rel_l == 0, mine_l, far_l)
        mine_r = jnp.where(same_r, own[h, :, 0:128, :], mate[h, :, 0:128, :])
        far_r = jnp.where(same_r, r1l[h], x1l[h])
        s2r[h] = jnp.where(rel_r == 0, mine_r, far_r)
        for c in second(h):
            c.start()
        if rounds == KVH:
            pl.semaphore_wait(near_sem.at[h, 0], 1)
            pl.semaphore_wait(near_sem.at[h, 1], 1)
        return reach * 2

    lax.fori_loop(0, KVH, prework, jnp.int32(1))

    def put(h):
        col = pl.ds(pl.multiple_of(h * QH, HD), QH)
        return pltpu.make_async_copy(dqv.at[:, col], dq_out.at[0, 0, :, col], out_sem.at[h])

    def main(h, carry):
        for c in second(h):
            c.wait_recv()
        kcol = pl.ds(pl.multiple_of(h * HD, HD), HD)
        near = jnp.where(same, own[h, :, 0:128, :], mate[h, :, 0:128, :])
        step1 = jnp.where(same, r1r[h], x1r[h])
        low = jnp.where(rel == 0, near, jnp.where(rel == 1, step1, jnp.where(rel == 3, r2l[h], r2r[h])))
        near = jnp.where(same, own[h, :, 128:256, :], mate[h, :, 128:256, :])
        step1 = jnp.where(same, r1l[h], x1l[h])
        high = jnp.where(rel == 0, near, jnp.where(rel == 3, step1, jnp.where(rel == 1, r2r[h], r2l[h])))
        kf[0:128] = low[0]
        kf[128:256] = high[0]
        kf[256:384] = kv[:, kcol]
        vf[0:128] = low[1]
        vf[128:256] = high[1]
        st[...] = dot(kf[0:256], qs[h], NT)
        dpt[...] = dot(vf[0:256], gs[h], NT)
        for g in range(GRP):
            c = pl.ds(g * ROWS, ROWS)
            s0 = jnp.where(ok0, st[0:128, c] * (SCALE * LOG2E), NEG)
            s1 = jnp.where(ok1, st[128:256, c] * (SCALE * LOG2E), NEG)
            s2 = ss[h, :, c]
            peak = jnp.max(jnp.maximum(jnp.maximum(s0, s1), s2), axis=0, keepdims=True)
            e0, e1, e2 = jnp.exp2(s0 - peak), jnp.exp2(s1 - peak), jnp.exp2(s2 - peak)
            inv = 1.0 / jnp.sum(e0 + e1 + e2, axis=0, keepdims=True)
            p0, p1, p2 = e0 * inv, e1 * inv, e2 * inv
            b0, b1_, b2_ = p0.astype(BF16), p1.astype(BF16), p2.astype(BF16)
            pb[0:128, c] = b0
            pb[128:256, c] = b1_
            pb[256:384, c] = b2_
            d0, d1, d2 = dpt[0:128, c], dpt[128:256, c], dps[h, :, c]
            delta = jnp.sum(b0.astype(F32) * d0 + b1_.astype(F32) * d1 + b2_.astype(F32) * d2,
                            axis=0, keepdims=True)
            ds[0:128, c] = (p0 * (d0 - delta)).astype(BF16)
            ds[128:256, c] = (p1 * (d1 - delta)).astype(BF16)
            ds[256:384, c] = (p2 * (d2 - delta)).astype(BF16)

        def note(n, line):
            share[n // 3, pl.ds(lax.rem(n, 3), 1), :] = jnp.sum(line, axis=0, keepdims=True)

        dv = dot(pb[...], gs[h], NN)
        note(KVH * GRP + h, dv)
        dk = dot(ds[...], qs[h], NN) * SCALE
        part[h, 0] = dk[0:256].astype(BF16)
        part[h, 1] = dv[0:256].astype(BF16)
        sl[h] = jnp.where(rel == 3, part[h, :, 0:128, :], part[h, :, 128:256, :])
        sr[h] = jnp.where(rel == 1, part[h, :, 128:256, :], part[h, :, 0:128, :])
        dkv[:, kcol] = dk[256:384].astype(BF16)
        dvv[:, kcol] = dv[256:384].astype(BF16)
        dq = dot(ds[...], kf[...], TN) * SCALE
        for g in range(GRP):
            col = pl.ds(pl.multiple_of(h * QH + g * HD, HD), HD)
            one = dq[g * ROWS:(g + 1) * ROWS]
            note(h * GRP + g, one)
            dqv[:, col] = one.astype(BF16)

        @pl.when(h < KVH - 1)
        def _():
            for c in back_first(h):
                c.start()
        put(h).start()
        return carry

    lax.fori_loop(0, KVH, main, 0)

    bias_out = [remote(share.at[lax.rem(r + o, 8)], b1.at[r], b1s.at[o - 1], b1r.at[o - 1], lax.rem(r + o, 8))
                for o in range(1, 8)]
    for c in bias_out:
        c.start()
    for c in back_first(KVH - 1):
        c.start()
    last = (pltpu.make_async_copy(dkv, dk_out.at[0, 0], out_sem.at[KVH]),
            pltpu.make_async_copy(dvv, dv_out.at[0, 0], out_sem.at[KVH + 1]))
    for c in last:
        c.start()
    b1[pl.ds(r, 1)] = share[pl.ds(r, 1)]

    def both(a, b):
        return jnp.logical_and(a, b)

    def pass_on(h):
        keep_m, a, b = back_first(h)
        a.wait_recv()
        b.wait_recv()
        for c in back_shared(h):
            c.start()
        keep_m.wait_recv()
        for c in back_shared(h):
            c.wait_recv()
        fr[h] = total(((both(rel == 1, same), part[h, :, 0:128, :]),
                       (both(rel_m == 1, same_m), pmate[h, :, 0:128, :]),
                       (both(rel_l == 1, same_l), zl[h]),
                       (both(rel_lx == 1, same_lx), xl[h]))).astype(BF16)
        fl[h] = total(((both(rel == 3, same), part[h, :, 128:256, :]),
                       (both(rel_m == 3, same_m), pmate[h, :, 128:256, :]),
                       (both(rel_r == 3, same_r), zr[h]),
                       (both(rel_rx == 3, same_rx), xr[h]))).astype(BF16)
        for c in back_second(h):
            c.start()

    def finish(h, carry):
        for c in back_second(h):
            c.wait_recv()
        col = pl.ds(pl.multiple_of(h * HD, HD), HD)
        low = total(((both(rel == 0, same), part[h, :, 0:128, :]),
                     (both(rel_m == 0, same_m), pmate[h, :, 0:128, :]),
                     (both(rel_r == 0, same_r), zr[h]),
                     (both(rel_rx == 0, same_rx), xr[h]))) + gl[h].astype(F32)
        high = total(((both(rel == 0, same), part[h, :, 128:256, :]),
                      (both(rel_m == 0, same_m), pmate[h, :, 128:256, :]),
                      (both(rel_l == 0, same_l), zl[h]),
                      (both(rel_lx == 0, same_lx), xl[h]))) + gr[h].astype(F32)
        kg[0:128, col] = low[0].astype(BF16)
        kg[128:256, col] = high[0].astype(BF16)
        vg[0:128, col] = low[1].astype(BF16)
        vg[128:256, col] = high[1].astype(BF16)
        return carry

    pass_on(0)
    for c in bias_out:
        c.wait_recv()
    row[...] = jnp.sum(b1[...], axis=0)[:, None, :]
    cross = [remote(row.at[lax.rem(xi + o, xs)], b2.at[xi], b2s.at[o - 1], b2r.at[o - 1],
                    lax.rem(xi + o, xs), "dp_0") for o in range(1, xs)]
    for c in cross:
        c.start()
    b2[pl.ds(xi, 1)] = row[pl.ds(xi, 1)]
    pass_on(1)
    for c in cross:
        c.wait_recv()
    zrow[...] = jnp.sum(b2[...], axis=0)

    def along(o):
        return remote(zrow, zall.at[zi], b3s.at[o - 1], b3r.at[o - 1], lax.rem(zi + o, zs), "dp_1")

    def along_start(o, carry):
        along(o).start()
        return carry

    lax.fori_loop(1, zs, along_start, 0)
    zall[pl.ds(zi, 1)] = zrow[...][None]
    pass_on(2)
    pass_on(3)
    lax.fori_loop(0, KVH, finish, 0)
    grads = (pltpu.make_async_copy(kg, pkg_out.at[0, 0], out_sem.at[KVH + 2]),
             pltpu.make_async_copy(vg, pvg_out.at[0, 0], out_sem.at[KVH + 3]))
    for c in grads:
        c.start()

    def along_wait(o, carry):
        along(o).wait_recv()
        return carry

    lax.fori_loop(1, zs, along_wait, 0)
    piece[pl.ds(xi, 1)] = (jnp.sum(zall[...], axis=0) * (1.0 / (8 * xs * zs)))[None]
    back = [remote(piece.at[xi], piece.at[xi], b4s.at[o - 1], b4r.at[o - 1], lax.rem(xi + o, xs), "dp_0")
            for o in range(1, xs)]
    for c in back:
        c.start()
    for c in back:
        c.wait_recv()
    sums[pl.ds(r, 1)] = piece[...].reshape(1, 4, HD)
    spread = [remote(sums.at[r], sums.at[r], b5s.at[o - 1], b5r.at[o - 1], lax.rem(r + o, 8))
              for o in range(1, 8)]
    for c in spread:
        c.start()

    for c in (*notes, *bias_out, *cross, *back):
        c.wait_send()

    def along_sent(o, carry):
        along(o).wait_send()
        return carry

    lax.fori_loop(1, zs, along_sent, 0)

    def drain(h, carry):
        for c in (*first(h), *shared(h), *second(h), *back_first(h), *back_shared(h), *back_second(h)):
            c.wait_send()
        put(h).wait()
        return carry

    lax.fori_loop(0, KVH, drain, 0)
    for c in (*last, *grads, *spread):
        c.wait()


def vmem(*shape, dtype=BF16):
    return pltpu.VMEM(shape, dtype)


def per_device(query, keys, vals, pk, pv, bias, grad, group, resp_len, blocks, keep):
    xs, zs = lax.axis_size("dp_0"), lax.axis_size("dp_1")
    smem = pl.BlockSpec(memory_space=pltpu.SMEM)
    anywhere = pl.BlockSpec(memory_space=pl.ANY)
    inside = pl.BlockSpec(memory_space=pltpu.VMEM)
    half = vmem(KVH, 2, 128, HD)
    whole = vmem(KVH, 2, 256, HD)
    wide = functools.partial(vmem, dtype=F32)
    dma = lambda *shape: pltpu.SemaphoreType.DMA(shape)
    out = jax.ShapeDtypeStruct
    *grads, sums = pl.pallas_call(
        functools.partial(kernel, xs, zs),
        out_shape=(out(query.shape, BF16), out(keys.shape, BF16), out(vals.shape, BF16),
                   out(pk.shape, BF16), out(pv.shape, BF16), out((8, 4, HD), F32)),
        in_specs=[smem] * 4 + [anywhere] * 5 + [inside] + [anywhere],
        out_specs=(anywhere,) * 5 + (inside,),
        scratch_shapes=[
            vmem(8, 8, HD, dtype=jnp.int32), whole, whole,
            half, half, half, half, half, half, half, half,
            vmem(ROWS, KVH * QH), vmem(ROWS, KVH * QH), vmem(ROWS, KVH * HD), vmem(ROWS, KVH * HD),
            vmem(KVH, QH, HD), vmem(KVH, QH, HD), wide(KVH, ROWS, QH), wide(KVH, ROWS, QH),
            wide(256, QH), wide(256, QH), vmem(384, HD), vmem(256, HD), vmem(384, QH), vmem(384, QH),
            vmem(ROWS, KVH * QH), vmem(ROWS, KVH * HD), vmem(ROWS, KVH * HD), whole,
            whole, half, half, half, half, half, half, half, half, half, half,
            vmem(256, KVH * HD), vmem(256, KVH * HD),
            wide(8, 4, HD), wide(8, 4, HD), wide(4, 1, HD), wide(xs, 1, HD), wide(1, HD),
            wide(zs, 1, HD), wide(4, 1, HD),
            dma(4), dma(KVH, 2), dma(KVH + 4), dma(7), dma(7), dma(7, KVH), dma(7, KVH),
            dma(7, KVH), dma(7, KVH), dma(7), dma(7), dma(3), dma(3), dma(zs), dma(zs),
            dma(3), dma(3), dma(7), dma(7), pltpu.SemaphoreType.REGULAR((KVH, 2)),
        ],
        compiler_params=pltpu.CompilerParams(collective_id=0, has_side_effects=True),
        name="attend",
    )(group, resp_len, blocks, keep, query, keys, vals, pk, pv, bias.reshape(1, -1), grad)
    flat = sums[:, :3].reshape(-1)
    return (*grads, flat[:KVH * QH], flat[KVH * QH:])


def solution(mesh):
    split = Mesh(mesh.devices.reshape(mesh.shape["resp"], 4, mesh.shape["dp"] // 4), ("resp", *DP))
    rows = P("resp", DP, None, None)
    in_specs = (rows, rows, rows, rows, rows, P(), rows,
                P("resp", DP), P("resp", DP), P("resp", DP), P("resp", DP, None))
    return jax.shard_map(per_device, mesh=split, in_specs=in_specs,
                         out_specs=(rows,) * 5 + (P(), P()), check_vma=False)
```

```python
import functools

import jax
import jax.numpy as jnp
from jax import lax
from jax.experimental import pallas as pl
from jax.experimental.pallas import tpu as pltpu
from jax.sharding import Mesh
from jax.sharding import PartitionSpec as P

HD = 128
ROWS = 128
KVH = 4
GRP = 5
QH = GRP * HD
CHIPS = 4
DP = ("dp_0", "dp_1")
AHEAD = 2
HELD = 2
NEG = -1e30
SCALE = HD ** (-0.5)
LOG2E = 1.4426950408889634
F32 = jnp.float32
BF16 = jnp.bfloat16
NT = (((1,), (1,)), ((), ()))
NN = (((1,), (0,)), ((), ()))
TN = (((0,), (0,)), ((), ()))


def dot(a, b, dims):
    return lax.dot_general(a, b, dims, preferred_element_type=F32)


def place():
    r = lax.axis_index("resp")
    y, core = r // 2, lax.rem(r, 2)
    left = lax.rem(y + CHIPS - 1, CHIPS)
    right = lax.rem(y + 1, CHIPS)
    return r, y, core, left, right


def remote(src, dst, send, recv, target):
    where = target if isinstance(target, dict) else {"resp": target}
    return pltpu.make_async_remote_copy(
        src_ref=src, dst_ref=dst, send_sem=send, recv_sem=recv,
        device_id=where, device_id_type=pl.DeviceIdType.MESH)


def tell(sem, target, axis="resp"):
    pl.semaphore_signal(sem, inc=1, device_id={axis: target}, device_id_type=pl.DeviceIdType.MESH)


def total(terms):
    out = 0.0
    for hit, x in terms:
        out = out + jnp.where(hit, x.astype(F32), 0.0)
    return out


def kernel(xs, zs, group_in, resp_len_in, blocks_in, keep_in, query, keys, vals, pk, pv, bias_in, grad,
           dq_out, dk_out, dv_out, pkg_out, pvg_out, sums,
           meta, own, mate, r1r, r1l, x1r, x1l, s2l, s2r, r2l, r2r,
           qv, gv, kv, vv, qs, gs, ss, dps, st, dpt, kf, vf, pb, ds, dqv, dkv, dvv, part,
           pmate, sl, sr, zr, zl, xr, xl, fr, fl, gl, gr, kg, vg,
           share, b1, zrow, zall, group, resp_len, blocks, keep, bias, bias_rows,
           in_sem, pre_sem, out_sem, msend, mrecv, csend, crecv, ssend, srecv,
           b1s, b1r, b3s, b3r, b5s, b5r, near_sem, plane_sem, int_sem):
    r, y, core, left, right = place()
    xi, zi = lax.axis_index("dp_0"), lax.axis_index("dp_1")
    mate_id = y * 2 + 1 - core
    left_id = left * 2 + core
    right_id = right * 2 + core
    rounds = max(zs.bit_length() - 2, 0)

    plane = r * xs + xi
    members = 8 * xs
    few = [pltpu.make_async_copy(a, b, int_sem.at[i]) for i, (a, b) in enumerate(
        ((group_in, group), (blocks_in, blocks), (resp_len_in, resp_len), (keep_in, keep), (bias_in, bias)))]
    for c in few:
        c.start()
    pre = []
    for h in range(KVH):
        col = pl.ds(h * HD, HD)
        pre.append(pltpu.make_async_copy(pk.at[0, 0, :, col], own.at[h, 0], pre_sem.at[h, 0]))
        pre.append(pltpu.make_async_copy(pv.at[0, 0, :, col], own.at[h, 1], pre_sem.at[h, 1]))
    for c in pre:
        c.start()
    loads = [pltpu.make_async_copy(a.at[0, 0], b, in_sem.at[i])
             for i, (a, b) in enumerate(((query, qv), (grad, gv), (keys, kv), (vals, vv)))]
    for c in loads:
        c.start()
    for c in few[:2]:
        c.wait()
    my_group = group[0, 0]
    meta[pl.ds(r, 1)] = jnp.full((1, 8, HD), my_group * 4 + blocks[0, 0], jnp.int32)
    share[...] = jnp.zeros_like(share)

    barrier = pltpu.get_barrier_semaphore()
    for o in range(1, 8):
        tell(barrier, lax.rem(r + o, 8))
    for o in range(1, xs):
        tell(barrier, lax.rem(xi + o, xs), "dp_0")
    if zs > 1:
        tell(barrier, lax.rem(zi + 1, zs), "dp_1")
        tell(barrier, lax.rem(zi + zs - 1, zs), "dp_1")
    pl.semaphore_wait(barrier, 7 + xs - 1 + (2 if zs > 1 else 0))

    notes = [remote(meta.at[r], meta.at[r], msend.at[o - 1], mrecv.at[o - 1], lax.rem(r + o, 8))
             for o in range(1, 8)]
    for c in notes:
        c.start()

    def lo(ref, h):
        return ref.at[h, :, pl.ds(0, 128), :]

    def hi(ref, h):
        return ref.at[h, :, pl.ds(128, 128), :]

    def first(h):
        return (remote(own.at[h], mate.at[h], csend.at[0, h], crecv.at[0, h], mate_id),
                remote(lo(own, h), r1r.at[h], csend.at[1, h], crecv.at[1, h], left_id),
                remote(hi(own, h), r1l.at[h], csend.at[2, h], crecv.at[2, h], right_id))

    def shared(h):
        return (remote(r1r.at[h], x1r.at[h], csend.at[3, h], crecv.at[3, h], mate_id),
                remote(r1l.at[h], x1l.at[h], csend.at[4, h], crecv.at[4, h], mate_id))

    def second(h):
        return (remote(s2l.at[h], r2r.at[h], csend.at[5, h], crecv.at[5, h], left_id),
                remote(s2r.at[h], r2l.at[h], csend.at[6, h], crecv.at[6, h], right_id))

    def back_first(h):
        return (remote(part.at[h], pmate.at[h], ssend.at[0, h], srecv.at[0, h], mate_id),
                remote(sl.at[h], zr.at[h], ssend.at[1, h], srecv.at[1, h], left_id),
                remote(sr.at[h], zl.at[h], ssend.at[2, h], srecv.at[2, h], right_id))

    def back_shared(h):
        return (remote(zr.at[h], xr.at[h], ssend.at[3, h], srecv.at[3, h], mate_id),
                remote(zl.at[h], xl.at[h], ssend.at[4, h], srecv.at[4, h], mate_id))

    def back_second(h):
        return (remote(fr.at[h], gl.at[h], ssend.at[5, h], srecv.at[5, h], right_id),
                remote(fl.at[h], gr.at[h], ssend.at[6, h], srecv.at[6, h], left_id))

    for h in range(KVH):
        pre[2 * h].wait()
        pre[2 * h + 1].wait()
        for c in first(h) if h < AHEAD else first(h)[:1]:
            c.start()
    for c in (*loads, *few[2:]):
        c.wait()
    for i in range(KVH * GRP // 2):
        pair = bias[i * 2 * HD:(i + 1) * 2 * HD].astype(F32)
        bias_rows[2 * i] = pair[:HD][None]
        bias_rows[2 * i + 1] = pair[HD:][None]
    for c in notes:
        c.wait_recv()

    info = [jnp.max(meta[i]) for i in range(8)]

    def look(idx):
        word = jnp.int32(0)
        for i in range(8):
            word = jnp.where(idx == i, info[i], word)
        return word

    def of(idx):
        g = look(idx) // 4
        return lax.rem(g // 2 - y + CHIPS, CHIPS), lax.rem(g, 2) == core

    holder_blocks = lax.rem(look(my_group), 4)
    rel, same = of(r)
    rel_m, same_m = of(mate_id)
    rel_l, same_l = of(left_id)
    rel_r, same_r = of(right_id)
    rel_lx, same_lx = of(left * 2 + 1 - core)
    rel_rx, same_rx = of(right * 2 + 1 - core)
    ok0 = keep[0, 0, 0] == 1
    ok1 = jnp.logical_and(holder_blocks > 1, keep[0, 0, 1] == 1)
    live = lax.broadcasted_iota(jnp.int32, (ROWS, HD), 0) < resp_len[0, 0]
    causal = (lax.broadcasted_iota(jnp.int32, (ROWS, ROWS), 0)
              <= lax.broadcasted_iota(jnp.int32, (ROWS, ROWS), 1))

    def prework(h, reach):
        if rounds == KVH:
            @pl.when(h == 0)
            def _():
                for o in range(1, 8):
                    tell(plane_sem, lax.rem(r + o, 8))
            tell(near_sem.at[h, 0], lax.rem(zi + reach, zs), "dp_1")
            tell(near_sem.at[h, 1], lax.rem(zi + zs - reach, zs), "dp_1")
        _, a, b = first(h)
        a.wait_recv()
        b.wait_recv()
        for c in shared(h):
            c.start()
        if AHEAD < KVH:
            @pl.when(h + AHEAD < KVH)
            def _():
                for c in first(h + AHEAD)[1:]:
                    c.start()
        for g in range(GRP):
            col = pl.ds(pl.multiple_of(h * QH + g * HD, HD), HD)
            rows = pl.ds(g * ROWS, ROWS)
            q = qv[:, col].astype(F32) + bias_rows[h * GRP + g]
            qs[h, rows, :] = q.astype(BF16)
            gs[h, rows, :] = jnp.where(live, gv[:, col].astype(F32), 0.0).astype(BF16)
        kcol = pl.ds(pl.multiple_of(h * HD, HD), HD)
        s = dot(kv[:, kcol], qs[h], NT) * (SCALE * LOG2E)
        for g in range(GRP):
            ss[h, :, g * ROWS:(g + 1) * ROWS] = jnp.where(
                causal, s[:, g * ROWS:(g + 1) * ROWS], NEG)
        dps[h] = dot(vv[:, kcol], gs[h], NT)
        first(h)[0].wait_recv()
        for c in shared(h):
            c.wait_recv()
        mine_l = jnp.where(same_l, own[h, :, 128:256, :], mate[h, :, 128:256, :])
        far_l = jnp.where(same_l, r1r[h], x1r[h])
        s2l[h] = jnp.where(rel_l == 0, mine_l, far_l)
        mine_r = jnp.where(same_r, own[h, :, 0:128, :], mate[h, :, 0:128, :])
        far_r = jnp.where(same_r, r1l[h], x1l[h])
        s2r[h] = jnp.where(rel_r == 0, mine_r, far_r)
        for c in second(h):
            c.start()
        if rounds == KVH:
            @pl.when(h == 0)
            def _():
                pl.semaphore_wait(plane_sem, 7)
            pl.semaphore_wait(near_sem.at[h, 0], 1)
            pl.semaphore_wait(near_sem.at[h, 1], 1)
        return reach * 2

    lax.fori_loop(0, KVH, prework, jnp.int32(1))

    def bias_out(o):
        to = lax.rem(plane + o, members)
        return remote(share.at[to], b1.at[plane], b1s.at[o - 1], b1r.at[o - 1],
                      {"resp": to // xs, "dp_0": lax.rem(to, xs)})

    def bias_start(o, carry):
        bias_out(o).start()
        return carry

    def bias_got(o, carry):
        bias_out(o).wait_recv()
        return carry

    def bias_sent(o, carry):
        bias_out(o).wait_send()
        return carry

    def put(h):
        col = pl.ds(pl.multiple_of(h * QH, HD), QH)
        return pltpu.make_async_copy(dqv.at[:, col], dq_out.at[0, 0, :, col], out_sem.at[h])

    def main(h, carry):
        for c in second(h):
            c.wait_recv()
        kcol = pl.ds(pl.multiple_of(h * HD, HD), HD)
        near = jnp.where(same, own[h, :, 0:128, :], mate[h, :, 0:128, :])
        step1 = jnp.where(same, r1r[h], x1r[h])
        low = jnp.where(rel == 0, near, jnp.where(rel == 1, step1, jnp.where(rel == 3, r2l[h], r2r[h])))
        near = jnp.where(same, own[h, :, 128:256, :], mate[h, :, 128:256, :])
        step1 = jnp.where(same, r1l[h], x1l[h])
        high = jnp.where(rel == 0, near, jnp.where(rel == 3, step1, jnp.where(rel == 1, r2r[h], r2l[h])))
        kf[0:128] = low[0]
        kf[128:256] = high[0]
        kf[256:384] = kv[:, kcol]
        vf[0:128] = low[1]
        vf[128:256] = high[1]
        st[...] = dot(kf[0:256], qs[h], NT)
        dpt[...] = dot(vf[0:256], gs[h], NT)
        for g in range(GRP):
            c = pl.ds(g * ROWS, ROWS)
            s0 = jnp.where(ok0, st[0:128, c] * (SCALE * LOG2E), NEG)
            s1 = jnp.where(ok1, st[128:256, c] * (SCALE * LOG2E), NEG)
            s2 = ss[h, :, c]
            peak = jnp.max(jnp.maximum(jnp.maximum(s0, s1), s2), axis=0, keepdims=True)
            e0, e1, e2 = jnp.exp2(s0 - peak), jnp.exp2(s1 - peak), jnp.exp2(s2 - peak)
            inv = 1.0 / jnp.sum(e0 + e1 + e2, axis=0, keepdims=True)
            p0, p1, p2 = e0 * inv, e1 * inv, e2 * inv
            b0, b1_, b2_ = p0.astype(BF16), p1.astype(BF16), p2.astype(BF16)
            pb[0:128, c] = b0
            pb[128:256, c] = b1_
            pb[256:384, c] = b2_
            d0, d1, d2 = dpt[0:128, c], dpt[128:256, c], dps[h, :, c]
            delta = jnp.sum(b0.astype(F32) * d0 + b1_.astype(F32) * d1 + b2_.astype(F32) * d2,
                            axis=0, keepdims=True)
            ds[0:128, c] = (p0 * (d0 - delta)).astype(BF16)
            ds[128:256, c] = (p1 * (d1 - delta)).astype(BF16)
            ds[256:384, c] = (p2 * (d2 - delta)).astype(BF16)

        def note(n, line):
            share[n // 3 * xs + lax.rem(n, 3)] = jnp.sum(line, axis=0, keepdims=True)

        dq = dot(ds[...], kf[...], TN) * SCALE
        for g in range(GRP):
            col = pl.ds(pl.multiple_of(h * QH + g * HD, HD), HD)
            one = dq[g * ROWS:(g + 1) * ROWS]
            note(h * GRP + g, one)
            dqv[:, col] = one.astype(BF16)
        dv = dot(pb[...], gs[h], NN)
        note(KVH * GRP + h, dv)
        part[h, 1] = dv[0:256].astype(BF16)
        dvv[:, kcol] = dv[256:384].astype(BF16)

        @pl.when(h == KVH - 1)
        def _():
            lax.fori_loop(1, members, bias_start, 0)

        dk = dot(ds[...], qs[h], NN) * SCALE
        part[h, 0] = dk[0:256].astype(BF16)
        dkv[:, kcol] = dk[256:384].astype(BF16)
        sl[h] = jnp.where(rel == 3, part[h, :, 0:128, :], part[h, :, 128:256, :])
        sr[h] = jnp.where(rel == 1, part[h, :, 128:256, :], part[h, :, 0:128, :])
        put(h).start()

        @pl.when(h < KVH - HELD)
        def _():
            for c in back_first(h):
                c.start()
        return carry

    lax.fori_loop(0, KVH, main, 0)

    last = (pltpu.make_async_copy(dkv, dk_out.at[0, 0], out_sem.at[KVH]),
            pltpu.make_async_copy(dvv, dv_out.at[0, 0], out_sem.at[KVH + 1]))
    for c in last:
        c.start()
    b1[pl.ds(plane, 1)] = share[pl.ds(plane, 1)]

    def both(a, b):
        return jnp.logical_and(a, b)

    def pass_on(h):
        keep_m, a, b = back_first(h)
        a.wait_recv()
        b.wait_recv()
        for c in back_shared(h):
            c.start()
        keep_m.wait_recv()
        for c in back_shared(h):
            c.wait_recv()
        fr[h] = total(((both(rel == 1, same), part[h, :, 0:128, :]),
                       (both(rel_m == 1, same_m), pmate[h, :, 0:128, :]),
                       (both(rel_l == 1, same_l), zl[h]),
                       (both(rel_lx == 1, same_lx), xl[h]))).astype(BF16)
        fl[h] = total(((both(rel == 3, same), part[h, :, 128:256, :]),
                       (both(rel_m == 3, same_m), pmate[h, :, 128:256, :]),
                       (both(rel_r == 3, same_r), zr[h]),
                       (both(rel_rx == 3, same_rx), xr[h]))).astype(BF16)
        for c in back_second(h):
            c.start()

    def finish(h, carry):
        for c in back_second(h):
            c.wait_recv()
        col = pl.ds(pl.multiple_of(h * HD, HD), HD)
        low = total(((both(rel == 0, same), part[h, :, 0:128, :]),
                     (both(rel_m == 0, same_m), pmate[h, :, 0:128, :]),
                     (both(rel_r == 0, same_r), zr[h]),
                     (both(rel_rx == 0, same_rx), xr[h]))) + gl[h].astype(F32)
        high = total(((both(rel == 0, same), part[h, :, 128:256, :]),
                      (both(rel_m == 0, same_m), pmate[h, :, 128:256, :]),
                      (both(rel_l == 0, same_l), zl[h]),
                      (both(rel_lx == 0, same_lx), xl[h]))) + gr[h].astype(F32)
        kg[0:128, col] = low[0].astype(BF16)
        kg[128:256, col] = high[0].astype(BF16)
        vg[0:128, col] = low[1].astype(BF16)
        vg[128:256, col] = high[1].astype(BF16)
        return carry

    lax.fori_loop(1, members, bias_got, 0)
    zrow[...] = jnp.sum(b1[...], axis=0)

    def along(o):
        return remote(zrow, zall.at[zi], b3s.at[o - 1], b3r.at[o - 1], {"dp_1": lax.rem(zi + o, zs)})

    def along_start(o, carry):
        along(o).start()
        return carry

    lax.fori_loop(1, zs, along_start, 0)
    for h in range(KVH - HELD, KVH):
        for c in back_first(h):
            c.start()
    zall[pl.ds(zi, 1)] = zrow[...][None]
    for h in range(KVH):
        pass_on(h)
    lax.fori_loop(0, KVH, finish, 0)
    grads = (pltpu.make_async_copy(kg, pkg_out.at[0, 0], out_sem.at[KVH + 2]),
             pltpu.make_async_copy(vg, pvg_out.at[0, 0], out_sem.at[KVH + 3]))
    for c in grads:
        c.start()

    def along_wait(o, carry):
        along(o).wait_recv()
        return carry

    lax.fori_loop(1, zs, along_wait, 0)
    sums[pl.ds(plane, 1)] = (jnp.sum(zall[...], axis=0) * (1.0 / (8 * xs * zs)))[None]

    def spread(o):
        to = lax.rem(plane + o, members)
        return remote(sums.at[plane], sums.at[plane], b5s.at[o - 1], b5r.at[o - 1],
                      {"resp": to // xs, "dp_0": lax.rem(to, xs)})

    def spread_start(o, carry):
        spread(o).start()
        return carry

    def spread_wait(o, carry):
        spread(o).wait()
        return carry

    lax.fori_loop(1, members, spread_start, 0)
    lax.fori_loop(1, members, bias_sent, 0)
    for c in notes:
        c.wait_send()

    def along_sent(o, carry):
        along(o).wait_send()
        return carry

    lax.fori_loop(1, zs, along_sent, 0)

    def drain(h, carry):
        for c in (*first(h), *shared(h), *second(h), *back_first(h), *back_shared(h), *back_second(h)):
            c.wait_send()
        put(h).wait()
        return carry

    lax.fori_loop(0, KVH, drain, 0)
    for c in (*last, *grads):
        c.wait()
    lax.fori_loop(1, members, spread_wait, 0)


def vmem(*shape, dtype=BF16):
    return pltpu.VMEM(shape, dtype)


def write_kernel(xs, a, b, c, d, e, sums, ao, bo, co, do, eo, qo, vo, at, bt, ct, dt, et, sem):
    moves = []
    for i, (src, mid, dst) in enumerate(((a, at, ao), (b, bt, bo), (c, ct, co), (d, dt, do), (e, et, eo))):
        if i == 0:
            n = mid.shape[0] // 4
            for j in range(4):
                part = pl.ds(j * n, n)
                moves.append((src.at[0, 0, part], mid.at[part], dst.at[0, 0, part]))
        else:
            moves.append((src.at[0, 0], mid, dst.at[0, 0]))
    into = [pltpu.make_async_copy(s, m, sem.at[0, i]) for i, (s, m, _) in enumerate(moves)]
    back = [pltpu.make_async_copy(m, t, sem.at[1, i]) for i, (_, m, t) in enumerate(moves)]
    for x in into:
        x.start()
    for n in range(KVH * GRP + KVH):
        line = sums[n // 3 * xs + n % 3, 0]
        if n < KVH * GRP:
            qo[pl.ds(n * HD, HD)] = line
        else:
            vo[pl.ds((n - KVH * GRP) * HD, HD)] = line
    for x, z in zip(into, back):
        x.wait()
        z.start()
    for z in back:
        z.wait()


def per_device(query, keys, vals, pk, pv, bias, grad, group, resp_len, blocks, keep):
    xs, zs = lax.axis_size("dp_0"), lax.axis_size("dp_1")
    members = 8 * xs
    smem_of = lambda *shape: pltpu.SMEM(shape, jnp.int32)
    anywhere = pl.BlockSpec(memory_space=pl.ANY)
    inside = pl.BlockSpec(memory_space=pltpu.VMEM)
    half = vmem(KVH, 2, 128, HD)
    whole = vmem(KVH, 2, 256, HD)
    wide = functools.partial(vmem, dtype=F32)
    dma = lambda *shape: pltpu.SemaphoreType.DMA(shape)
    out = jax.ShapeDtypeStruct
    *grads, sums = pl.pallas_call(
        functools.partial(kernel, xs, zs),
        out_shape=(out(query.shape, BF16), out(keys.shape, BF16), out(vals.shape, BF16),
                   out(pk.shape, BF16), out(pv.shape, BF16), out((members, 1, HD), F32)),
        in_specs=[pl.BlockSpec(memory_space=pltpu.HBM)] * 4 + [anywhere] * 7,
        out_specs=(anywhere,) * 5 + (inside,),
        scratch_shapes=[
            vmem(8, 8, HD, dtype=jnp.int32), whole, whole,
            half, half, half, half, half, half, half, half,
            vmem(ROWS, KVH * QH), vmem(ROWS, KVH * QH), vmem(ROWS, KVH * HD), vmem(ROWS, KVH * HD),
            vmem(KVH, QH, HD), vmem(KVH, QH, HD), wide(KVH, ROWS, QH), wide(KVH, ROWS, QH),
            wide(256, QH), wide(256, QH), vmem(384, HD), vmem(256, HD), vmem(384, QH), vmem(384, QH),
            vmem(ROWS, KVH * QH), vmem(ROWS, KVH * HD), vmem(ROWS, KVH * HD), whole,
            whole, half, half, half, half, half, half, half, half, half, half,
            vmem(256, KVH * HD), vmem(256, KVH * HD),
            wide(members, 1, HD), wide(members, 1, HD), wide(1, HD), wide(zs, 1, HD),
            smem_of(1, 1), smem_of(1, 1), smem_of(1, 1), smem_of(1, 1, 2), vmem(KVH * QH), wide(KVH * GRP, 1, HD),
            dma(4), dma(KVH, 2), dma(KVH + 4), dma(7), dma(7), dma(7, KVH), dma(7, KVH),
            dma(7, KVH), dma(7, KVH), dma(members), dma(members), dma(zs), dma(zs),
            dma(members), dma(members), pltpu.SemaphoreType.REGULAR((KVH, 2)),
            pltpu.SemaphoreType.REGULAR, dma(5),
        ],
        compiler_params=pltpu.CompilerParams(collective_id=0, has_side_effects=True),
        name="attend",
    )(group, resp_len, blocks, keep, query, keys, vals, pk, pv, bias, grad)
    shapes = [out(g.shape, BF16) for g in grads]
    return pl.pallas_call(
        functools.partial(write_kernel, xs),
        out_shape=(*shapes, out((KVH * QH,), F32), out((KVH * HD,), F32)),
        in_specs=[anywhere] * 5 + [inside],
        out_specs=(anywhere,) * 5 + (inside, inside),
        scratch_shapes=[vmem(*g.shape[2:]) for g in grads] + [dma(2, 8)],
        name="write",
    )(*grads, sums)


def solution(mesh):
    split = Mesh(mesh.devices.reshape(mesh.shape["resp"], 4, mesh.shape["dp"] // 4), ("resp", *DP))
    rows = P("resp", DP, None, None)
    in_specs = (rows, rows, rows, rows, rows, P(), rows,
                P("resp", DP), P("resp", DP), P("resp", DP), P("resp", DP, None))
    return jax.shard_map(per_device, mesh=split, in_specs=in_specs,
                         out_specs=(rows,) * 5 + (P(), P()), check_vma=False)
```

```python
import functools

import jax
import jax.numpy as jnp
from jax import lax
from jax.experimental import pallas as pl
from jax.experimental.pallas import tpu as pltpu
from jax.sharding import Mesh
from jax.sharding import PartitionSpec as P

HD = 128
ROWS = 128
KVH = 4
GRP = 5
QH = GRP * HD
CHIPS = 4
DP = ("dp_0", "dp_1")
HELD = 2
NEG = -1e30
SCALE = HD ** (-0.5)
LOG2E = 1.4426950408889634
F32 = jnp.float32
BF16 = jnp.bfloat16
NT = (((1,), (1,)), ((), ()))
NN = (((1,), (0,)), ((), ()))
TN = (((0,), (0,)), ((), ()))


def dot(a, b, dims):
    return lax.dot_general(a, b, dims, preferred_element_type=F32)


def place():
    r = lax.axis_index("resp")
    y, core = r // 2, lax.rem(r, 2)
    left = lax.rem(y + CHIPS - 1, CHIPS)
    right = lax.rem(y + 1, CHIPS)
    return r, y, core, left, right


def remote(src, dst, send, recv, target):
    where = target if isinstance(target, dict) else {"resp": target}
    return pltpu.make_async_remote_copy(
        src_ref=src, dst_ref=dst, send_sem=send, recv_sem=recv,
        device_id=where, device_id_type=pl.DeviceIdType.MESH)


def tell(sem, target, axis="resp"):
    pl.semaphore_signal(sem, inc=1, device_id={axis: target}, device_id_type=pl.DeviceIdType.MESH)


def total(terms):
    out = 0.0
    for hit, x in terms:
        out = out + jnp.where(hit, x.astype(F32), 0.0)
    return out


def kernel(xs, zs, group_in, resp_len_in, blocks_in, keep_in, query, keys, vals, pk, pv, bias_in, grad,
           dq_out, dk_out, dv_out, pkg_out, pvg_out, sums,
           meta, own, mate, r1r, r1l, x1r, x1l, s2l, s2r, r2l, r2r,
           qv, gv, kv, vv, qs, gs, ss, dps, st, dpt, kf, vf, pb, ds, dqv, dkv, dvv, part,
           pmate, sl, sr, zr, zl, xr, xl, fr, fl, gl, gr, kg, vg,
           share, b1, zrow, zall, group, resp_len, blocks, keep, bias, bias_rows,
           in_sem, pre_sem, out_sem, msend, mrecv, csend, crecv, ssend, srecv,
           b1s, b1r, b3s, b3r, b5s, b5r, near_sem, plane_sem, int_sem):
    r, y, core, left, right = place()
    xi, zi = lax.axis_index("dp_0"), lax.axis_index("dp_1")
    mate_id = y * 2 + 1 - core
    left_id = left * 2 + core
    right_id = right * 2 + core
    rounds = max(zs.bit_length() - 2, 0)

    plane = r * xs + xi
    members = 8 * xs
    barrier = pltpu.get_barrier_semaphore()
    for o in range(1, 8):
        tell(barrier, lax.rem(r + o, 8))
    for o in range(1, xs):
        tell(barrier, lax.rem(xi + o, xs), "dp_0")
    if zs > 1:
        tell(barrier, lax.rem(zi + 1, zs), "dp_1")
        tell(barrier, lax.rem(zi + zs - 1, zs), "dp_1")
    few = [pltpu.make_async_copy(a, b, int_sem.at[i]) for i, (a, b) in enumerate(
        ((group_in, group), (blocks_in, blocks), (resp_len_in, resp_len), (keep_in, keep), (bias_in, bias)))]
    for c in few:
        c.start()
    pre = []
    for h in range(KVH):
        col = pl.ds(h * HD, HD)
        pre.append(pltpu.make_async_copy(pk.at[0, 0, :, col], own.at[h, 0], pre_sem.at[h, 0]))
        pre.append(pltpu.make_async_copy(pv.at[0, 0, :, col], own.at[h, 1], pre_sem.at[h, 1]))
    for c in pre:
        c.start()
    loads = [pltpu.make_async_copy(a.at[0, 0], b, in_sem.at[i])
             for i, (a, b) in enumerate(((query, qv), (grad, gv), (keys, kv), (vals, vv)))]
    for c in loads:
        c.start()
    for c in few[:2]:
        c.wait()
    my_group = group[0, 0]
    meta[pl.ds(r, 1)] = jnp.full((1, 8, HD), my_group * 4 + blocks[0, 0], jnp.int32)
    share[...] = jnp.zeros_like(share)

    pl.semaphore_wait(barrier, 7 + xs - 1 + (2 if zs > 1 else 0))

    def near_tell(i):
        if i < rounds:
            tell(near_sem.at[i, 0], lax.rem(zi + 2 ** i, zs), "dp_1")
            tell(near_sem.at[i, 1], lax.rem(zi + zs - 2 ** i, zs), "dp_1")

    def near_wait(i):
        if i < rounds:
            pl.semaphore_wait(near_sem.at[i, 0], 1)
            pl.semaphore_wait(near_sem.at[i, 1], 1)

    notes = [remote(meta.at[r], meta.at[r], msend.at[o - 1], mrecv.at[o - 1], lax.rem(r + o, 8))
             for o in range(1, 8)]
    for c in notes:
        c.start()

    def lo(ref, h):
        return ref.at[h, :, pl.ds(0, 128), :]

    def hi(ref, h):
        return ref.at[h, :, pl.ds(128, 128), :]

    def first(h):
        return (remote(own.at[h], mate.at[h], csend.at[0, h], crecv.at[0, h], mate_id),
                remote(lo(own, h), r1r.at[h], csend.at[1, h], crecv.at[1, h], left_id),
                remote(hi(own, h), r1l.at[h], csend.at[2, h], crecv.at[2, h], right_id))

    def shared(h):
        return (remote(r1r.at[h], x1r.at[h], csend.at[3, h], crecv.at[3, h], mate_id),
                remote(r1l.at[h], x1l.at[h], csend.at[4, h], crecv.at[4, h], mate_id))

    def second(h):
        return (remote(s2l.at[h], r2r.at[h], csend.at[5, h], crecv.at[5, h], left_id),
                remote(s2r.at[h], r2l.at[h], csend.at[6, h], crecv.at[6, h], right_id))

    def back_first(h):
        return (remote(part.at[h], pmate.at[h], ssend.at[0, h], srecv.at[0, h], mate_id),
                remote(sl.at[h], zr.at[h], ssend.at[1, h], srecv.at[1, h], left_id),
                remote(sr.at[h], zl.at[h], ssend.at[2, h], srecv.at[2, h], right_id))

    def back_shared(h):
        return (remote(zr.at[h], xr.at[h], ssend.at[3, h], srecv.at[3, h], mate_id),
                remote(zl.at[h], xl.at[h], ssend.at[4, h], srecv.at[4, h], mate_id))

    def back_second(h):
        return (remote(fr.at[h], gl.at[h], ssend.at[5, h], srecv.at[5, h], right_id),
                remote(fl.at[h], gr.at[h], ssend.at[6, h], srecv.at[6, h], left_id))

    for h in range(KVH):
        pre[2 * h].wait()
        pre[2 * h + 1].wait()
        for c in first(h) if h < 2 else first(h)[:1]:
            c.start()
    near_tell(0)
    for o in range(1, 8):
        tell(plane_sem, lax.rem(r + o, 8))
    for c in (*loads, *few[2:]):
        c.wait()
    for i in range(KVH * GRP // 2):
        pair = bias[i * 2 * HD:(i + 1) * 2 * HD].astype(F32)
        bias_rows[2 * i] = pair[:HD][None]
        bias_rows[2 * i + 1] = pair[HD:][None]
    live = lax.broadcasted_iota(jnp.int32, (ROWS, HD), 0) < resp_len[0, 0]
    causal = (lax.broadcasted_iota(jnp.int32, (ROWS, ROWS), 0)
              <= lax.broadcasted_iota(jnp.int32, (ROWS, ROWS), 1))

    def local(h, carry):
        for g in range(GRP):
            col = pl.ds(pl.multiple_of(h * QH + g * HD, HD), HD)
            rows = pl.ds(g * ROWS, ROWS)
            q = qv[:, col].astype(F32) + bias_rows[h * GRP + g]
            qs[h, rows, :] = q.astype(BF16)
            gs[h, rows, :] = jnp.where(live, gv[:, col].astype(F32), 0.0).astype(BF16)
        kcol = pl.ds(pl.multiple_of(h * HD, HD), HD)
        s = dot(kv[:, kcol], qs[h], NT) * (SCALE * LOG2E)
        for g in range(GRP):
            ss[h, :, g * ROWS:(g + 1) * ROWS] = jnp.where(
                causal, s[:, g * ROWS:(g + 1) * ROWS], NEG)
        dps[h] = dot(vv[:, kcol], gs[h], NT)
        return carry

    def arrive(h):
        for c in first(h)[1:]:
            c.wait_recv()
        for c in shared(h):
            c.start()

    lax.fori_loop(0, 2, local, 0)
    for h in (0, 1):
        for c in first(h)[1:]:
            c.wait_send()
    for h in (2, 3):
        for c in first(h)[1:]:
            c.start()
    pl.semaphore_wait(plane_sem, 7)
    near_wait(0)
    near_tell(1)
    local(2, 0)
    arrive(0)
    arrive(1)
    local(3, 0)
    for c in notes:
        c.wait_recv()

    info = [jnp.max(meta[i]) for i in range(8)]

    def look(idx):
        word = jnp.int32(0)
        for i in range(8):
            word = jnp.where(idx == i, info[i], word)
        return word

    def of(idx):
        g = look(idx) // 4
        return lax.rem(g // 2 - y + CHIPS, CHIPS), lax.rem(g, 2) == core

    holder_blocks = lax.rem(look(my_group), 4)
    rel, same = of(r)
    rel_m, same_m = of(mate_id)
    rel_l, same_l = of(left_id)
    rel_r, same_r = of(right_id)
    rel_lx, same_lx = of(left * 2 + 1 - core)
    rel_rx, same_rx = of(right * 2 + 1 - core)
    ok0 = keep[0, 0, 0] == 1
    ok1 = jnp.logical_and(holder_blocks > 1, keep[0, 0, 1] == 1)
    def forward(h):
        first(h)[0].wait_recv()
        for c in shared(h):
            c.wait_recv()
        mine_l = jnp.where(same_l, own[h, :, 128:256, :], mate[h, :, 128:256, :])
        far_l = jnp.where(same_l, r1r[h], x1r[h])
        s2l[h] = jnp.where(rel_l == 0, mine_l, far_l)
        mine_r = jnp.where(same_r, own[h, :, 0:128, :], mate[h, :, 0:128, :])
        far_r = jnp.where(same_r, r1l[h], x1l[h])
        s2r[h] = jnp.where(rel_r == 0, mine_r, far_r)
        for c in second(h):
            c.start()

    forward(0)
    forward(1)
    near_wait(1)
    near_tell(2)
    arrive(2)
    arrive(3)
    forward(2)
    forward(3)

    def bias_out(o):
        to = lax.rem(plane + o, members)
        return remote(share.at[to], b1.at[plane], b1s.at[o - 1], b1r.at[o - 1],
                      {"resp": to // xs, "dp_0": lax.rem(to, xs)})

    def bias_start(o, carry):
        bias_out(o).start()
        return carry

    def bias_got(o, carry):
        bias_out(o).wait_recv()
        return carry

    def bias_sent(o, carry):
        bias_out(o).wait_send()
        return carry

    def put(h):
        col = pl.ds(pl.multiple_of(h * QH, HD), QH)
        return pltpu.make_async_copy(dqv.at[:, col], dq_out.at[0, 0, :, col], out_sem.at[h])

    def main(h, carry):
        for c in second(h):
            c.wait_recv()
        kcol = pl.ds(pl.multiple_of(h * HD, HD), HD)
        near = jnp.where(same, own[h, :, 0:128, :], mate[h, :, 0:128, :])
        step1 = jnp.where(same, r1r[h], x1r[h])
        low = jnp.where(rel == 0, near, jnp.where(rel == 1, step1, jnp.where(rel == 3, r2l[h], r2r[h])))
        near = jnp.where(same, own[h, :, 128:256, :], mate[h, :, 128:256, :])
        step1 = jnp.where(same, r1l[h], x1l[h])
        high = jnp.where(rel == 0, near, jnp.where(rel == 3, step1, jnp.where(rel == 1, r2r[h], r2l[h])))
        kf[0:128] = low[0]
        kf[128:256] = high[0]
        kf[256:384] = kv[:, kcol]

        @pl.when(h == 1)
        def _():
            near_wait(2)
            near_tell(3)

        vf[0:128] = low[1]
        vf[128:256] = high[1]
        st[...] = dot(kf[0:256], qs[h], NT)
        dpt[...] = dot(vf[0:256], gs[h], NT)
        for g in range(GRP):
            c = pl.ds(g * ROWS, ROWS)
            s0 = jnp.where(ok0, st[0:128, c] * (SCALE * LOG2E), NEG)
            s1 = jnp.where(ok1, st[128:256, c] * (SCALE * LOG2E), NEG)
            s2 = ss[h, :, c]
            peak = jnp.max(jnp.maximum(jnp.maximum(s0, s1), s2), axis=0, keepdims=True)
            e0, e1, e2 = jnp.exp2(s0 - peak), jnp.exp2(s1 - peak), jnp.exp2(s2 - peak)
            inv = 1.0 / jnp.sum(e0 + e1 + e2, axis=0, keepdims=True)
            p0, p1, p2 = e0 * inv, e1 * inv, e2 * inv
            b0, b1_, b2_ = p0.astype(BF16), p1.astype(BF16), p2.astype(BF16)
            pb[0:128, c] = b0
            pb[128:256, c] = b1_
            pb[256:384, c] = b2_
            d0, d1, d2 = dpt[0:128, c], dpt[128:256, c], dps[h, :, c]
            delta = jnp.sum(b0.astype(F32) * d0 + b1_.astype(F32) * d1 + b2_.astype(F32) * d2,
                            axis=0, keepdims=True)
            ds[0:128, c] = (p0 * (d0 - delta)).astype(BF16)
            ds[128:256, c] = (p1 * (d1 - delta)).astype(BF16)
            ds[256:384, c] = (p2 * (d2 - delta)).astype(BF16)

        def note(n, line):
            share[n // 3 * xs + lax.rem(n, 3)] = jnp.sum(line, axis=0, keepdims=True)

        dq = dot(ds[...], kf[...], TN) * SCALE
        for g in range(GRP):
            col = pl.ds(pl.multiple_of(h * QH + g * HD, HD), HD)
            one = dq[g * ROWS:(g + 1) * ROWS]
            note(h * GRP + g, one)
            dqv[:, col] = one.astype(BF16)
        dv = dot(pb[...], gs[h], NN)
        note(KVH * GRP + h, dv)
        part[h, 1] = dv[0:256].astype(BF16)
        dvv[:, kcol] = dv[256:384].astype(BF16)

        @pl.when(h == KVH - 1)
        def _():
            lax.fori_loop(1, members, bias_start, 0)

        dk = dot(ds[...], qs[h], NN) * SCALE
        part[h, 0] = dk[0:256].astype(BF16)
        dkv[:, kcol] = dk[256:384].astype(BF16)
        sl[h] = jnp.where(rel == 3, part[h, :, 0:128, :], part[h, :, 128:256, :])
        sr[h] = jnp.where(rel == 1, part[h, :, 128:256, :], part[h, :, 0:128, :])
        put(h).start()

        @pl.when(h < KVH - HELD)
        def _():
            for c in back_first(h):
                c.start()
        return carry

    lax.fori_loop(0, KVH, main, 0)

    last = (pltpu.make_async_copy(dkv, dk_out.at[0, 0], out_sem.at[KVH]),
            pltpu.make_async_copy(dvv, dv_out.at[0, 0], out_sem.at[KVH + 1]))
    for c in last:
        c.start()
    b1[pl.ds(plane, 1)] = share[pl.ds(plane, 1)]

    def both(a, b):
        return jnp.logical_and(a, b)

    def pass_on(h):
        keep_m, a, b = back_first(h)
        a.wait_recv()
        b.wait_recv()
        for c in back_shared(h):
            c.start()
        keep_m.wait_recv()
        for c in back_shared(h):
            c.wait_recv()
        fr[h] = total(((both(rel == 1, same), part[h, :, 0:128, :]),
                       (both(rel_m == 1, same_m), pmate[h, :, 0:128, :]),
                       (both(rel_l == 1, same_l), zl[h]),
                       (both(rel_lx == 1, same_lx), xl[h]))).astype(BF16)
        fl[h] = total(((both(rel == 3, same), part[h, :, 128:256, :]),
                       (both(rel_m == 3, same_m), pmate[h, :, 128:256, :]),
                       (both(rel_r == 3, same_r), zr[h]),
                       (both(rel_rx == 3, same_rx), xr[h]))).astype(BF16)
        for c in back_second(h):
            c.start()

    def finish(h, carry):
        for c in back_second(h):
            c.wait_recv()
        col = pl.ds(pl.multiple_of(h * HD, HD), HD)
        low = total(((both(rel == 0, same), part[h, :, 0:128, :]),
                     (both(rel_m == 0, same_m), pmate[h, :, 0:128, :]),
                     (both(rel_r == 0, same_r), zr[h]),
                     (both(rel_rx == 0, same_rx), xr[h]))) + gl[h].astype(F32)
        high = total(((both(rel == 0, same), part[h, :, 128:256, :]),
                      (both(rel_m == 0, same_m), pmate[h, :, 128:256, :]),
                      (both(rel_l == 0, same_l), zl[h]),
                      (both(rel_lx == 0, same_lx), xl[h]))) + gr[h].astype(F32)
        kg[0:128, col] = low[0].astype(BF16)
        kg[128:256, col] = high[0].astype(BF16)
        vg[0:128, col] = low[1].astype(BF16)
        vg[128:256, col] = high[1].astype(BF16)
        return carry

    lax.fori_loop(1, members, bias_got, 0)
    near_wait(3)
    zrow[...] = jnp.sum(b1[...], axis=0)

    def along(o):
        return remote(zrow, zall.at[zi], b3s.at[o - 1], b3r.at[o - 1], {"dp_1": lax.rem(zi + o, zs)})

    def along_start(o, carry):
        along(o).start()
        return carry

    lax.fori_loop(1, zs, along_start, 0)
    for h in range(KVH - HELD, KVH):
        for c in back_first(h):
            c.start()
    zall[pl.ds(zi, 1)] = zrow[...][None]
    for h in range(KVH):
        pass_on(h)
    lax.fori_loop(0, KVH, finish, 0)
    grads = (pltpu.make_async_copy(kg, pkg_out.at[0, 0], out_sem.at[KVH + 2]),
             pltpu.make_async_copy(vg, pvg_out.at[0, 0], out_sem.at[KVH + 3]))
    for c in grads:
        c.start()

    def along_wait(o, carry):
        along(o).wait_recv()
        return carry

    lax.fori_loop(1, zs, along_wait, 0)
    sums[pl.ds(plane, 1)] = (jnp.sum(zall[...], axis=0) * (1.0 / (8 * xs * zs)))[None]

    def spread(o):
        to = lax.rem(plane + o, members)
        return remote(sums.at[plane], sums.at[plane], b5s.at[o - 1], b5r.at[o - 1],
                      {"resp": to // xs, "dp_0": lax.rem(to, xs)})

    def spread_start(o, carry):
        spread(o).start()
        return carry

    def spread_wait(o, carry):
        spread(o).wait()
        return carry

    lax.fori_loop(1, members, spread_start, 0)
    lax.fori_loop(1, members, bias_sent, 0)
    for c in notes:
        c.wait_send()

    def along_sent(o, carry):
        along(o).wait_send()
        return carry

    lax.fori_loop(1, zs, along_sent, 0)

    def drain(h, carry):
        for c in (first(h)[0], *shared(h), *second(h), *back_first(h), *back_shared(h), *back_second(h)):
            c.wait_send()
        put(h).wait()
        return carry

    lax.fori_loop(0, KVH, drain, 0)
    for h in (2, 3):
        for c in first(h)[1:]:
            c.wait_send()
    for c in (*last, *grads):
        c.wait()
    lax.fori_loop(1, members, spread_wait, 0)


def vmem(*shape, dtype=BF16):
    return pltpu.VMEM(shape, dtype)


def write_kernel(xs, a, b, c, d, e, sums, ao, bo, co, do, eo, qo, vo, at, bt, ct, dt, et, st, qt, vt, sem):
    moves = []
    for i, (src, mid, dst) in enumerate(((a, at, ao), (b, bt, bo), (c, ct, co), (d, dt, do), (e, et, eo))):
        if i == 0:
            n = mid.shape[0] // 4
            for j in range(4):
                part = pl.ds(j * n, n)
                moves.append((src.at[0, 0, part], mid.at[part], dst.at[0, 0, part]))
        else:
            moves.append((src.at[0, 0], mid, dst.at[0, 0]))
    table = pltpu.make_async_copy(sums, st, sem.at[0, 8])
    table.start()
    into = [pltpu.make_async_copy(s, m, sem.at[0, i]) for i, (s, m, _) in enumerate(moves)]
    back = [pltpu.make_async_copy(m, t, sem.at[1, i]) for i, (_, m, t) in enumerate(moves)]
    rows = [pltpu.make_async_copy(qt, qo, sem.at[1, 8]), pltpu.make_async_copy(vt, vo, sem.at[1, 9])]
    for x in into:
        x.start()
    table.wait()
    for n in range(KVH * GRP + KVH):
        line = st[n // 3 * xs + n % 3, 0]
        if n < KVH * GRP:
            qt[pl.ds(n * HD, HD)] = line
        else:
            vt[pl.ds((n - KVH * GRP) * HD, HD)] = line
    for x in rows:
        x.start()
    for x, z in zip(into, back):
        x.wait()
        z.start()
    for z in (*back, *rows):
        z.wait()


def per_device(query, keys, vals, pk, pv, bias, grad, group, resp_len, blocks, keep):
    xs, zs = lax.axis_size("dp_0"), lax.axis_size("dp_1")
    members = 8 * xs
    smem_of = lambda *shape: pltpu.SMEM(shape, jnp.int32)
    anywhere = pl.BlockSpec(memory_space=pl.ANY)
    inside = pl.BlockSpec(memory_space=pltpu.VMEM)
    half = vmem(KVH, 2, 128, HD)
    whole = vmem(KVH, 2, 256, HD)
    wide = functools.partial(vmem, dtype=F32)
    dma = lambda *shape: pltpu.SemaphoreType.DMA(shape)
    out = jax.ShapeDtypeStruct
    *grads, sums = pl.pallas_call(
        functools.partial(kernel, xs, zs),
        out_shape=(out(query.shape, BF16), out(keys.shape, BF16), out(vals.shape, BF16),
                   out(pk.shape, BF16), out(pv.shape, BF16), out((members, 1, HD), F32)),
        in_specs=[anywhere] * 11,
        out_specs=(anywhere,) * 5 + (inside,),
        scratch_shapes=[
            vmem(8, 8, HD, dtype=jnp.int32), whole, whole,
            half, half, half, half, half, half, half, half,
            vmem(ROWS, KVH * QH), vmem(ROWS, KVH * QH), vmem(ROWS, KVH * HD), vmem(ROWS, KVH * HD),
            vmem(KVH, QH, HD), vmem(KVH, QH, HD), wide(KVH, ROWS, QH), wide(KVH, ROWS, QH),
            wide(256, QH), wide(256, QH), vmem(384, HD), vmem(256, HD), vmem(384, QH), vmem(384, QH),
            vmem(ROWS, KVH * QH), vmem(ROWS, KVH * HD), vmem(ROWS, KVH * HD), whole,
            whole, half, half, half, half, half, half, half, half, half, half,
            vmem(256, KVH * HD), vmem(256, KVH * HD),
            wide(members, 1, HD), wide(members, 1, HD), wide(1, HD), wide(zs, 1, HD),
            smem_of(1, 1), smem_of(1, 1), smem_of(1, 1), smem_of(1, 1, 2), vmem(KVH * QH), wide(KVH * GRP, 1, HD),
            dma(4), dma(KVH, 2), dma(KVH + 4), dma(7), dma(7), dma(7, KVH), dma(7, KVH),
            dma(7, KVH), dma(7, KVH), dma(members), dma(members), dma(zs), dma(zs),
            dma(members), dma(members), pltpu.SemaphoreType.REGULAR((KVH, 2)),
            pltpu.SemaphoreType.REGULAR, dma(5),
        ],
        compiler_params=pltpu.CompilerParams(collective_id=0, has_side_effects=True),
        name="attend",
    )(group, resp_len, blocks, keep, query, keys, vals, pk, pv, bias, grad)
    shapes = [out(g.shape, BF16) for g in grads]
    return pl.pallas_call(
        functools.partial(write_kernel, xs),
        out_shape=(*shapes, out((KVH * QH,), F32), out((KVH * HD,), F32)),
        in_specs=[anywhere] * 6,
        out_specs=(anywhere,) * 7,
        scratch_shapes=[vmem(*g.shape[2:]) for g in grads] + [
            wide(members, 1, HD), wide(KVH * GRP * HD), wide(KVH * HD), dma(2, 10)],
        name="write",
    )(*grads, sums)


def solution(mesh):
    split = Mesh(mesh.devices.reshape(mesh.shape["resp"], 4, mesh.shape["dp"] // 4), ("resp", *DP))
    rows = P("resp", DP, None, None)
    in_specs = (rows, rows, rows, rows, rows, P(), rows,
                P("resp", DP), P("resp", DP), P("resp", DP), P("resp", DP, None))
    return jax.shard_map(per_device, mesh=split, in_specs=in_specs,
                         out_specs=(rows,) * 5 + (P(), P()), check_vma=False)
```

```python
import functools

import jax
import jax.numpy as jnp
from jax import lax
from jax.experimental import pallas as pl
from jax.experimental.pallas import tpu as pltpu
from jax.sharding import Mesh
from jax.sharding import PartitionSpec as P

HD = 128
ROWS = 128
KVH = 4
GRP = 5
QH = GRP * HD
CHIPS = 4
DP = ("dp_0", "dp_1")
HELD = 2
NEG = -1e30
SCALE = HD ** (-0.5)
LOG2E = 1.4426950408889634
F32 = jnp.float32
BF16 = jnp.bfloat16
NT = (((1,), (1,)), ((), ()))
NN = (((1,), (0,)), ((), ()))
TN = (((0,), (0,)), ((), ()))


def dot(a, b, dims):
    return lax.dot_general(a, b, dims, preferred_element_type=F32)


def place():
    r = lax.axis_index("resp")
    y, core = r // 2, lax.rem(r, 2)
    left = lax.rem(y + CHIPS - 1, CHIPS)
    right = lax.rem(y + 1, CHIPS)
    return r, y, core, left, right


def remote(src, dst, send, recv, target):
    where = target if isinstance(target, dict) else {"resp": target}
    return pltpu.make_async_remote_copy(
        src_ref=src, dst_ref=dst, send_sem=send, recv_sem=recv,
        device_id=where, device_id_type=pl.DeviceIdType.MESH)


def tell(sem, target, axis="resp"):
    pl.semaphore_signal(sem, inc=1, device_id={axis: target}, device_id_type=pl.DeviceIdType.MESH)


def outward(i, n):
    return n // 2 + (i + 1) // 2 * (1 - 2 * lax.rem(i, 2))


def total(terms):
    out = 0.0
    for hit, x in terms:
        out = out + jnp.where(hit, x.astype(F32), 0.0)
    return out


def kernel(xs, zs, group_in, resp_len_in, blocks_in, keep_in, query, keys, vals, pk, pv, bias_in, grad,
           dq_out, dk_out, dv_out, pkg_out, pvg_out, sums,
           meta, own, mate, r1r, r1l, x1r, x1l, s2l, s2r, r2l, r2r,
           qv, gv, kv, vv, qs, gs, ss, dps, st, dpt, kf, vf, pb, ds, dqv, dkv, dvv, part,
           pmate, sl, sr, zr, zl, xr, xl, fr, fl, gl, gr, kg, vg,
           share, b1, zrow, zall, group, resp_len, blocks, keep, bias, bias_rows,
           in_sem, pre_sem, out_sem, msend, mrecv, csend, crecv, ssend, srecv,
           b1s, b1r, b3s, b3r, b5s, b5r, near_sem, plane_sem, int_sem):
    r, y, core, left, right = place()
    xi, zi = lax.axis_index("dp_0"), lax.axis_index("dp_1")
    mate_id = y * 2 + 1 - core
    left_id = left * 2 + core
    right_id = right * 2 + core
    rounds = max(zs.bit_length() - 2, 0)

    plane = r * xs + xi
    members = 8 * xs
    barrier = pltpu.get_barrier_semaphore()
    for o in range(1, 8):
        tell(barrier, lax.rem(r + o, 8))
    for o in range(1, xs):
        tell(barrier, lax.rem(xi + o, xs), "dp_0")
    if zs > 1:
        tell(barrier, lax.rem(zi + 1, zs), "dp_1")
        tell(barrier, lax.rem(zi + zs - 1, zs), "dp_1")
    few = [pltpu.make_async_copy(a, b, int_sem.at[i]) for i, (a, b) in enumerate(
        ((group_in, group), (blocks_in, blocks), (resp_len_in, resp_len), (keep_in, keep), (bias_in, bias)))]
    for c in few:
        c.start()
    pre = []
    for h in range(KVH):
        col = pl.ds(h * HD, HD)
        pre.append(pltpu.make_async_copy(pk.at[0, 0, :, col], own.at[h, 0], pre_sem.at[h, 0]))
        pre.append(pltpu.make_async_copy(pv.at[0, 0, :, col], own.at[h, 1], pre_sem.at[h, 1]))
    for c in pre:
        c.start()
    loads = [pltpu.make_async_copy(a.at[0, 0], b, in_sem.at[i])
             for i, (a, b) in enumerate(((query, qv), (grad, gv), (keys, kv), (vals, vv)))]
    for c in loads:
        c.start()
    for c in few[:2]:
        c.wait()
    my_group = group[0, 0]
    meta[pl.ds(r, 1)] = jnp.full((1, 8, HD), my_group * 4 + blocks[0, 0], jnp.int32)
    share[...] = jnp.zeros_like(share)

    pl.semaphore_wait(barrier, 7 + xs - 1 + (2 if zs > 1 else 0))

    def near_tell(i):
        if i < rounds:
            tell(near_sem.at[i, 0], lax.rem(zi + 2 ** i, zs), "dp_1")
            tell(near_sem.at[i, 1], lax.rem(zi + zs - 2 ** i, zs), "dp_1")

    def near_wait(i):
        if i < rounds:
            pl.semaphore_wait(near_sem.at[i, 0], 1)
            pl.semaphore_wait(near_sem.at[i, 1], 1)

    notes = [remote(meta.at[r], meta.at[r], msend.at[o - 1], mrecv.at[o - 1], lax.rem(r + o, 8))
             for o in range(1, 8)]
    for c in notes:
        c.start()

    def lo(ref, h):
        return ref.at[h, :, pl.ds(0, 128), :]

    def hi(ref, h):
        return ref.at[h, :, pl.ds(128, 128), :]

    def first(h):
        return (remote(own.at[h], mate.at[h], csend.at[0, h], crecv.at[0, h], mate_id),
                remote(lo(own, h), r1r.at[h], csend.at[1, h], crecv.at[1, h], left_id),
                remote(hi(own, h), r1l.at[h], csend.at[2, h], crecv.at[2, h], right_id))

    def shared(h):
        return (remote(r1r.at[h], x1r.at[h], csend.at[3, h], crecv.at[3, h], mate_id),
                remote(r1l.at[h], x1l.at[h], csend.at[4, h], crecv.at[4, h], mate_id))

    def second(h):
        return (remote(s2l.at[h], r2r.at[h], csend.at[5, h], crecv.at[5, h], left_id),
                remote(s2r.at[h], r2l.at[h], csend.at[6, h], crecv.at[6, h], right_id))

    def back_first(h):
        return (remote(part.at[h], pmate.at[h], ssend.at[0, h], srecv.at[0, h], mate_id),
                remote(sl.at[h], zr.at[h], ssend.at[1, h], srecv.at[1, h], left_id),
                remote(sr.at[h], zl.at[h], ssend.at[2, h], srecv.at[2, h], right_id))

    def back_shared(h):
        return (remote(zr.at[h], xr.at[h], ssend.at[3, h], srecv.at[3, h], mate_id),
                remote(zl.at[h], xl.at[h], ssend.at[4, h], srecv.at[4, h], mate_id))

    def back_second(h):
        return (remote(fr.at[h], gl.at[h], ssend.at[5, h], srecv.at[5, h], right_id),
                remote(fl.at[h], gr.at[h], ssend.at[6, h], srecv.at[6, h], left_id))

    for h in range(KVH):
        pre[2 * h].wait()
        pre[2 * h + 1].wait()
        for c in first(h) if h < 2 else first(h)[:1]:
            c.start()
    near_tell(0)
    for o in range(1, 8):
        tell(plane_sem, lax.rem(r + o, 8))
    for c in (*loads, *few[2:]):
        c.wait()
    for i in range(KVH * GRP // 2):
        pair = bias[i * 2 * HD:(i + 1) * 2 * HD].astype(F32)
        bias_rows[2 * i] = pair[:HD][None]
        bias_rows[2 * i + 1] = pair[HD:][None]
    live = lax.broadcasted_iota(jnp.int32, (ROWS, HD), 0) < resp_len[0, 0]
    causal = (lax.broadcasted_iota(jnp.int32, (ROWS, ROWS), 0)
              <= lax.broadcasted_iota(jnp.int32, (ROWS, ROWS), 1))

    def local(h, carry):
        for g in range(GRP):
            col = pl.ds(pl.multiple_of(h * QH + g * HD, HD), HD)
            rows = pl.ds(g * ROWS, ROWS)
            q = qv[:, col].astype(F32) + bias_rows[h * GRP + g]
            qs[h, rows, :] = q.astype(BF16)
            gs[h, rows, :] = jnp.where(live, gv[:, col].astype(F32), 0.0).astype(BF16)
        kcol = pl.ds(pl.multiple_of(h * HD, HD), HD)
        s = dot(kv[:, kcol], qs[h], NT) * (SCALE * LOG2E)
        for g in range(GRP):
            ss[h, :, g * ROWS:(g + 1) * ROWS] = jnp.where(
                causal, s[:, g * ROWS:(g + 1) * ROWS], NEG)
        dps[h] = dot(vv[:, kcol], gs[h], NT)
        return carry

    def arrive(h):
        for c in first(h)[1:]:
            c.wait_recv()
        for c in shared(h):
            c.start()

    lax.fori_loop(0, 2, local, 0)
    for h in (0, 1):
        for c in first(h)[1:]:
            c.wait_send()
    for h in (2, 3):
        for c in first(h)[1:]:
            c.start()
    pl.semaphore_wait(plane_sem, 7)
    near_wait(0)
    near_tell(1)
    local(2, 0)
    for c in notes:
        c.wait_recv()

    info = [jnp.max(meta[i]) for i in range(8)]

    def look(idx):
        word = jnp.int32(0)
        for i in range(8):
            word = jnp.where(idx == i, info[i], word)
        return word

    def of(idx):
        g = look(idx) // 4
        return lax.rem(g // 2 - y + CHIPS, CHIPS), lax.rem(g, 2) == core

    holder_blocks = lax.rem(look(my_group), 4)
    rel, same = of(r)
    rel_m, same_m = of(mate_id)
    rel_l, same_l = of(left_id)
    rel_r, same_r = of(right_id)
    rel_lx, same_lx = of(left * 2 + 1 - core)
    rel_rx, same_rx = of(right * 2 + 1 - core)
    ok0 = keep[0, 0, 0] == 1
    ok1 = jnp.logical_and(holder_blocks > 1, keep[0, 0, 1] == 1)
    arrive(0)
    arrive(1)
    local(3, 0)
    def forward(h):
        first(h)[0].wait_recv()
        for c in shared(h):
            c.wait_recv()
        mine_l = jnp.where(same_l, own[h, :, 128:256, :], mate[h, :, 128:256, :])
        far_l = jnp.where(same_l, r1r[h], x1r[h])
        s2l[h] = jnp.where(rel_l == 0, mine_l, far_l)
        mine_r = jnp.where(same_r, own[h, :, 0:128, :], mate[h, :, 0:128, :])
        far_r = jnp.where(same_r, r1l[h], x1l[h])
        s2r[h] = jnp.where(rel_r == 0, mine_r, far_r)
        for c in second(h):
            c.start()

    forward(0)
    forward(1)
    near_wait(1)
    near_tell(2)
    arrive(2)
    arrive(3)
    forward(2)
    forward(3)

    def bias_out(o):
        to = lax.rem(plane + o, members)
        return remote(share.at[to], b1.at[plane], b1s.at[o - 1], b1r.at[o - 1],
                      {"resp": to // xs, "dp_0": lax.rem(to, xs)})

    def bias_start(o, carry):
        bias_out(outward(o, members)).start()
        return carry

    def bias_got(o, carry):
        bias_out(o).wait_recv()
        return carry

    def bias_sent(o, carry):
        bias_out(o).wait_send()
        return carry

    def put(h):
        col = pl.ds(pl.multiple_of(h * QH, HD), QH)
        return pltpu.make_async_copy(dqv.at[:, col], dq_out.at[0, 0, :, col], out_sem.at[h])

    def main(h, carry):
        for c in second(h):
            c.wait_recv()
        kcol = pl.ds(pl.multiple_of(h * HD, HD), HD)
        near = jnp.where(same, own[h, :, 0:128, :], mate[h, :, 0:128, :])
        step1 = jnp.where(same, r1r[h], x1r[h])
        low = jnp.where(rel == 0, near, jnp.where(rel == 1, step1, jnp.where(rel == 3, r2l[h], r2r[h])))
        near = jnp.where(same, own[h, :, 128:256, :], mate[h, :, 128:256, :])
        step1 = jnp.where(same, r1l[h], x1l[h])
        high = jnp.where(rel == 0, near, jnp.where(rel == 3, step1, jnp.where(rel == 1, r2r[h], r2l[h])))
        kf[0:128] = low[0]
        kf[128:256] = high[0]
        kf[256:384] = kv[:, kcol]

        @pl.when(h == 1)
        def _():
            near_wait(2)
            near_tell(3)

        vf[0:128] = low[1]
        vf[128:256] = high[1]
        st[...] = dot(kf[0:256], qs[h], NT)
        dpt[...] = dot(vf[0:256], gs[h], NT)
        for g in range(GRP):
            c = pl.ds(g * ROWS, ROWS)
            s0 = jnp.where(ok0, st[0:128, c] * (SCALE * LOG2E), NEG)
            s1 = jnp.where(ok1, st[128:256, c] * (SCALE * LOG2E), NEG)
            s2 = ss[h, :, c]
            peak = jnp.max(jnp.maximum(jnp.maximum(s0, s1), s2), axis=0, keepdims=True)
            e0, e1, e2 = jnp.exp2(s0 - peak), jnp.exp2(s1 - peak), jnp.exp2(s2 - peak)
            inv = 1.0 / jnp.sum(e0 + e1 + e2, axis=0, keepdims=True)
            p0, p1, p2 = e0 * inv, e1 * inv, e2 * inv
            b0, b1_, b2_ = p0.astype(BF16), p1.astype(BF16), p2.astype(BF16)
            pb[0:128, c] = b0
            pb[128:256, c] = b1_
            pb[256:384, c] = b2_
            d0, d1, d2 = dpt[0:128, c], dpt[128:256, c], dps[h, :, c]
            delta = jnp.sum(b0.astype(F32) * d0 + b1_.astype(F32) * d1 + b2_.astype(F32) * d2,
                            axis=0, keepdims=True)
            ds[0:128, c] = (p0 * (d0 - delta)).astype(BF16)
            ds[128:256, c] = (p1 * (d1 - delta)).astype(BF16)
            ds[256:384, c] = (p2 * (d2 - delta)).astype(BF16)

        def note(n, line):
            share[n // 3 * xs + lax.rem(n, 3)] = jnp.sum(line, axis=0, keepdims=True)

        dq = dot(ds[...], kf[...], TN) * SCALE
        for g in range(GRP):
            col = pl.ds(pl.multiple_of(h * QH + g * HD, HD), HD)
            one = dq[g * ROWS:(g + 1) * ROWS]
            note(h * GRP + g, one)
            dqv[:, col] = one.astype(BF16)
        dv = dot(pb[...], gs[h], NN)
        note(KVH * GRP + h, dv)
        part[h, 1] = dv[0:256].astype(BF16)
        dvv[:, kcol] = dv[256:384].astype(BF16)

        @pl.when(h == KVH - 1)
        def _():
            lax.fori_loop(0, members - 1, bias_start, 0)

        dk = dot(ds[...], qs[h], NN) * SCALE
        part[h, 0] = dk[0:256].astype(BF16)
        dkv[:, kcol] = dk[256:384].astype(BF16)
        sl[h] = jnp.where(rel == 3, part[h, :, 0:128, :], part[h, :, 128:256, :])
        sr[h] = jnp.where(rel == 1, part[h, :, 128:256, :], part[h, :, 0:128, :])
        put(h).start()

        @pl.when(h < KVH - HELD)
        def _():
            for c in back_first(h):
                c.start()
        return carry

    lax.fori_loop(0, KVH, main, 0)

    last = (pltpu.make_async_copy(dkv, dk_out.at[0, 0], out_sem.at[KVH]),
            pltpu.make_async_copy(dvv, dv_out.at[0, 0], out_sem.at[KVH + 1]))
    for c in last:
        c.start()
    b1[pl.ds(plane, 1)] = share[pl.ds(plane, 1)]

    def both(a, b):
        return jnp.logical_and(a, b)

    def pass_on(h):
        keep_m, a, b = back_first(h)
        a.wait_recv()
        b.wait_recv()
        for c in back_shared(h):
            c.start()
        keep_m.wait_recv()
        for c in back_shared(h):
            c.wait_recv()
        fr[h] = total(((both(rel == 1, same), part[h, :, 0:128, :]),
                       (both(rel_m == 1, same_m), pmate[h, :, 0:128, :]),
                       (both(rel_l == 1, same_l), zl[h]),
                       (both(rel_lx == 1, same_lx), xl[h]))).astype(BF16)
        fl[h] = total(((both(rel == 3, same), part[h, :, 128:256, :]),
                       (both(rel_m == 3, same_m), pmate[h, :, 128:256, :]),
                       (both(rel_r == 3, same_r), zr[h]),
                       (both(rel_rx == 3, same_rx), xr[h]))).astype(BF16)
        for c in back_second(h):
            c.start()

    def finish(h, carry):
        for c in back_second(h):
            c.wait_recv()
        col = pl.ds(pl.multiple_of(h * HD, HD), HD)
        low = total(((both(rel == 0, same), part[h, :, 0:128, :]),
                     (both(rel_m == 0, same_m), pmate[h, :, 0:128, :]),
                     (both(rel_r == 0, same_r), zr[h]),
                     (both(rel_rx == 0, same_rx), xr[h]))) + gl[h].astype(F32)
        high = total(((both(rel == 0, same), part[h, :, 128:256, :]),
                      (both(rel_m == 0, same_m), pmate[h, :, 128:256, :]),
                      (both(rel_l == 0, same_l), zl[h]),
                      (both(rel_lx == 0, same_lx), xl[h]))) + gr[h].astype(F32)
        kg[0:128, col] = low[0].astype(BF16)
        kg[128:256, col] = high[0].astype(BF16)
        vg[0:128, col] = low[1].astype(BF16)
        vg[128:256, col] = high[1].astype(BF16)
        return carry

    lax.fori_loop(1, members, bias_got, 0)
    near_wait(3)
    zrow[...] = jnp.sum(b1[...], axis=0)

    def along(o):
        return remote(zrow, zall.at[zi], b3s.at[o - 1], b3r.at[o - 1], {"dp_1": lax.rem(zi + o, zs)})

    def along_start(o, carry):
        along(outward(o, zs)).start()
        return carry

    lax.fori_loop(0, zs - 1, along_start, 0)
    for h in range(KVH - HELD, KVH):
        for c in back_first(h):
            c.start()
    zall[pl.ds(zi, 1)] = zrow[...][None]
    for h in range(KVH):
        pass_on(h)
    lax.fori_loop(0, KVH, finish, 0)
    grads = (pltpu.make_async_copy(kg, pkg_out.at[0, 0], out_sem.at[KVH + 2]),
             pltpu.make_async_copy(vg, pvg_out.at[0, 0], out_sem.at[KVH + 3]))
    for c in grads:
        c.start()

    def along_wait(o, carry):
        along(o).wait_recv()
        return carry

    lax.fori_loop(1, zs, along_wait, 0)
    sums[pl.ds(plane, 1)] = (jnp.sum(zall[...], axis=0) * (1.0 / (8 * xs * zs)))[None]

    def spread(o):
        to = lax.rem(plane + o, members)
        return remote(sums.at[plane], sums.at[plane], b5s.at[o - 1], b5r.at[o - 1],
                      {"resp": to // xs, "dp_0": lax.rem(to, xs)})

    def spread_start(o, carry):
        spread(outward(o, members)).start()
        return carry

    def spread_wait(o, carry):
        spread(o).wait()
        return carry

    lax.fori_loop(0, members - 1, spread_start, 0)
    lax.fori_loop(1, members, bias_sent, 0)
    for c in notes:
        c.wait_send()

    def along_sent(o, carry):
        along(o).wait_send()
        return carry

    lax.fori_loop(1, zs, along_sent, 0)

    def drain(h, carry):
        for c in (first(h)[0], *shared(h), *second(h), *back_first(h), *back_shared(h), *back_second(h)):
            c.wait_send()
        put(h).wait()
        return carry

    lax.fori_loop(0, KVH, drain, 0)
    for h in (2, 3):
        for c in first(h)[1:]:
            c.wait_send()
    for c in (*last, *grads):
        c.wait()
    lax.fori_loop(1, members, spread_wait, 0)


def vmem(*shape, dtype=BF16):
    return pltpu.VMEM(shape, dtype)


def write_kernel(xs, a, b, c, d, e, sums, ao, bo, co, do, eo, qo, vo, at, bt, ct, dt, et, st, qt, vt, sem):
    moves = []
    for i, (src, mid, dst) in enumerate(((a, at, ao), (b, bt, bo), (c, ct, co), (d, dt, do), (e, et, eo))):
        if i == 0:
            n = mid.shape[0] // 4
            for j in range(4):
                part = pl.ds(j * n, n)
                moves.append((src.at[0, 0, part], mid.at[part], dst.at[0, 0, part]))
        else:
            moves.append((src.at[0, 0], mid, dst.at[0, 0]))
    table = pltpu.make_async_copy(sums, st, sem.at[0, 8])
    table.start()
    into = [pltpu.make_async_copy(s, m, sem.at[0, i]) for i, (s, m, _) in enumerate(moves)]
    back = [pltpu.make_async_copy(m, t, sem.at[1, i]) for i, (_, m, t) in enumerate(moves)]
    rows = [pltpu.make_async_copy(qt, qo, sem.at[1, 8]), pltpu.make_async_copy(vt, vo, sem.at[1, 9])]
    for x in into:
        x.start()
    table.wait()
    for n in range(KVH * GRP + KVH):
        line = st[n // 3 * xs + n % 3, 0]
        if n < KVH * GRP:
            qt[pl.ds(n * HD, HD)] = line
        else:
            vt[pl.ds((n - KVH * GRP) * HD, HD)] = line
    for x in rows:
        x.start()
    for x, z in zip(into, back):
        x.wait()
        z.start()
    for z in (*back, *rows):
        z.wait()


def per_device(query, keys, vals, pk, pv, bias, grad, group, resp_len, blocks, keep):
    xs, zs = lax.axis_size("dp_0"), lax.axis_size("dp_1")
    members = 8 * xs
    smem_of = lambda *shape: pltpu.SMEM(shape, jnp.int32)
    anywhere = pl.BlockSpec(memory_space=pl.ANY)
    inside = pl.BlockSpec(memory_space=pltpu.VMEM)
    half = vmem(KVH, 2, 128, HD)
    whole = vmem(KVH, 2, 256, HD)
    wide = functools.partial(vmem, dtype=F32)
    dma = lambda *shape: pltpu.SemaphoreType.DMA(shape)
    out = jax.ShapeDtypeStruct
    *grads, sums = pl.pallas_call(
        functools.partial(kernel, xs, zs),
        out_shape=(out(query.shape, BF16), out(keys.shape, BF16), out(vals.shape, BF16),
                   out(pk.shape, BF16), out(pv.shape, BF16), out((members, 1, HD), F32)),
        in_specs=[anywhere] * 11,
        out_specs=(anywhere,) * 5 + (inside,),
        scratch_shapes=[
            vmem(8, 8, HD, dtype=jnp.int32), whole, whole,
            half, half, half, half, half, half, half, half,
            vmem(ROWS, KVH * QH), vmem(ROWS, KVH * QH), vmem(ROWS, KVH * HD), vmem(ROWS, KVH * HD),
            vmem(KVH, QH, HD), vmem(KVH, QH, HD), wide(KVH, ROWS, QH), wide(KVH, ROWS, QH),
            wide(256, QH), wide(256, QH), vmem(384, HD), vmem(256, HD), vmem(384, QH), vmem(384, QH),
            vmem(ROWS, KVH * QH), vmem(ROWS, KVH * HD), vmem(ROWS, KVH * HD), whole,
            whole, half, half, half, half, half, half, half, half, half, half,
            vmem(256, KVH * HD), vmem(256, KVH * HD),
            wide(members, 1, HD), wide(members, 1, HD), wide(1, HD), wide(zs, 1, HD),
            smem_of(1, 1), smem_of(1, 1), smem_of(1, 1), smem_of(1, 1, 2), vmem(KVH * QH), wide(KVH * GRP, 1, HD),
            dma(4), dma(KVH, 2), dma(KVH + 4), dma(7), dma(7), dma(7, KVH), dma(7, KVH),
            dma(7, KVH), dma(7, KVH), dma(members), dma(members), dma(zs), dma(zs),
            dma(members), dma(members), pltpu.SemaphoreType.REGULAR((KVH, 2)),
            pltpu.SemaphoreType.REGULAR, dma(5),
        ],
        compiler_params=pltpu.CompilerParams(collective_id=0, has_side_effects=True),
        name="attend",
    )(group, resp_len, blocks, keep, query, keys, vals, pk, pv, bias, grad)
    shapes = [out(g.shape, BF16) for g in grads]
    return pl.pallas_call(
        functools.partial(write_kernel, xs),
        out_shape=(*shapes, out((KVH * QH,), F32), out((KVH * HD,), F32)),
        in_specs=[anywhere] * 6,
        out_specs=(anywhere,) * 7,
        scratch_shapes=[vmem(*g.shape[2:]) for g in grads] + [
            wide(members, 1, HD), wide(KVH * GRP * HD), wide(KVH * HD), dma(2, 10)],
        name="write",
    )(*grads, sums)


def solution(mesh):
    split = Mesh(mesh.devices.reshape(mesh.shape["resp"], 4, mesh.shape["dp"] // 4), ("resp", *DP))
    rows = P("resp", DP, None, None)
    in_specs = (rows, rows, rows, rows, rows, P(), rows,
                P("resp", DP), P("resp", DP), P("resp", DP), P("resp", DP, None))
    return jax.shard_map(per_device, mesh=split, in_specs=in_specs,
                         out_specs=(rows,) * 5 + (P(), P()), check_vma=False)
```
